32 devices in a mesh: groups: 2 (over x), ctx: 16 (over z, y, core).
Axes of the slice: x: 2, y: 2, z: 4, core: 2. Of those that a mesh axis runs over, the one named last changes fastest.
Arguments:
- queries: bfloat16 [12288, 1024], P(('groups', 'ctx')), parts along dimension 0
- keys: bfloat16 [12288, 1024], P(('groups', 'ctx')), parts along dimension 0
- values: bfloat16 [12288, 1024], P(('groups', 'ctx')), parts along dimension 0, may hold values from -6 to 6
- out_weight: bfloat16 [1024, 1024], P('ctx'), may hold values from -0.1875 to 0.1875
- grad_output: bfloat16 [12288, 1024], P(('groups', 'ctx')), parts along dimension 0, may hold values from -6 to 6
- complex_id: int32 [12288], P('groups'), parts along dimension 0, may hold values from 0 to 3, never falling along the last dimension, each value on 1 to 3072 neighbouring positions
- contacts: int32 [96, 6], P(('groups', 'ctx')), parts along dimension 0, may hold values from 0 to 47, as said below
- contact_count: int32 [96], P(('groups', 'ctx')), parts along dimension 0, may hold values from 3 to 6, as said below
Outputs:
- mixed: bfloat16 [12288, 1024], P(('groups', 'ctx')), parts along dimension 0
- grad_queries: bfloat16 [12288, 1024], P(('groups', 'ctx')), parts along dimension 0
- grad_keys: bfloat16 [12288, 1024], P(('groups', 'ctx')), parts along dimension 0
- grad_values: bfloat16 [12288, 1024], P(('groups', 'ctx')), parts along dimension 0
- grad_weight: float32 [2048, 1024], P(('groups', 'ctx')), parts along dimension 0
The draws below stay inside these ranges and needn't reach their ends.
There are 2 independent parts, one for each index of `groups`. The reference program is written for one: setup_inputs(seed, part) draws one part's arguments, and reference() takes and returns one part's arrays. A program takes and returns all parts, laid end to end along the dimension named above; an argument that names none is the same for every part. Nothing has to cross between parts.
Inputs may be any that keep to these rules, and one draw needn't show every extreme that they name: `contacts`: entry 0 of each list is the query block itself; the other entries are distinct blocks, other than the query block, at most 6 blocks from it. `contact_count`: on some device every block of the device has all 6 entries live.
All inputs are finite; a program needn't handle non-finite values.
Results may differ from the reference program's by a relative error of at most 0.022.
Values may be sent and summed in bfloat16 or wider, within the bound.
A program may use at most 192 MiB of HBM per device.

```python
import math
import jax
import jax.numpy as jnp
import numpy as np
from jax import lax

HEADS = 16
D = 1024
BLOCKS_DEV = 3
LISTED = 6
TOK_DEV = 384
TOKENS = 6144
AMINO_TILE_COUNT = 48
NEIGHBOR_RADIUS = 6
N_CTX = 16


def query_key_pair(key):
    key_query = jax.random.fold_in(key, 101)
    key_keys = jax.random.fold_in(key, 202)
    queries_out = jax.random.normal(key_query, (TOKENS, D), jnp.float32)
    keys_out = jax.random.normal(key_keys, (TOKENS, D), jnp.float32)
    return (queries_out, keys_out)


def draw_queries(key, part):
    return query_key_pair(key)[0].astype(jnp.bfloat16)


def draw_keys(key, part):
    return query_key_pair(key)[1].astype(jnp.bfloat16)


def draw_contacts(key, part):
    generator_state = jax.random.fold_in(key, 11)
    key_up = jax.random.fold_in(key, 12)
    key_down = jax.random.fold_in(key, 13)
    blocks = jnp.arange(AMINO_TILE_COUNT, dtype=jnp.int32)
    offsets = jnp.concatenate([jnp.arange(-NEIGHBOR_RADIUS, 0, dtype=jnp.int32), jnp.arange(1, NEIGHBOR_RADIUS + 1, dtype=jnp.int32)])
    target = blocks[:, None] + offsets[None, :]
    inside = (target >= 0) & (target < AMINO_TILE_COUNT)
    partner_tile_index = jnp.arange(2 * NEIGHBOR_RADIUS, dtype=jnp.int32)[None, :]
    higher_partner_pick = NEIGHBOR_RADIUS + jax.random.randint(key_up, (AMINO_TILE_COUNT, 1), 0, NEIGHBOR_RADIUS)
    lower_partner_pick = jax.random.randint(key_down, (AMINO_TILE_COUNT, 1), 0, NEIGHBOR_RADIUS)
    logit_increment = jnp.where(partner_tile_index == higher_partner_pick, 1 << 27, 0) + jnp.where(partner_tile_index == lower_partner_pick, 1 << 26, 0)
    similarity_logits = jax.random.randint(generator_state, (AMINO_TILE_COUNT, 2 * NEIGHBOR_RADIUS), 0, 1 << 20) * (2 * NEIGHBOR_RADIUS) + partner_tile_index + logit_increment
    similarity_logits = jnp.where(inside, similarity_logits, -1 - partner_tile_index)
    chosen = lax.top_k(similarity_logits, LISTED - 1)[1]
    picked = jnp.take_along_axis(target, chosen, axis=1)
    return jnp.concatenate([blocks[:, None], picked], axis=1).astype(jnp.int32)


def draw_contact_count(key, part):
    devices = AMINO_TILE_COUNT // BLOCKS_DEV
    key_heavy = jax.random.fold_in(key, 7)
    key_forced = jax.random.fold_in(key, 8)
    key_light = jax.random.fold_in(key, 9)
    heavy = jax.random.randint(key_heavy, (devices,), 0, 4) == 0
    forced = jax.random.randint(key_forced, (), 0, devices)
    heavy = heavy | (jnp.arange(devices, dtype=jnp.int32) == forced)
    low = min(3, LISTED)
    light = jax.random.randint(key_light, (AMINO_TILE_COUNT,), low, max(low, LISTED // 2 + 1) + 1)
    heavy_rows = jnp.repeat(heavy, BLOCKS_DEV)
    return jnp.where(heavy_rows, LISTED, light).astype(jnp.int32)


def levels(stream_key, shape, cuts, least, top_value):
    def one(dim, blocks):
        steps = jax.random.uniform(jax.random.fold_in(jax.random.fold_in(stream_key, 6), dim), (blocks,), jnp.float32, least / len(cuts), top_value / len(cuts))
        return jnp.repeat(jnp.exp(steps), shape[dim] // blocks).reshape((-1,) + (1,) * (len(shape) - dim - 1))

    factor_of = one(*cuts[0])
    for cut in cuts[1:]:
        factor_of = factor_of * one(*cut)
    return factor_of


def split_up(number_of, total, reach, skew):
    loads = [(1 << 20) // math.isqrt(grade ** skew) + 1 for grade in range(2, number_of + 1)]
    surplus, counts = total - reach - (number_of - 1), [1] * (number_of - 1)
    while surplus > 0:
        candidates = [i for i in range(number_of - 1) if counts[i] < reach]
        pool, remaining = sum([loads[i] for i in candidates]), surplus
        for i in candidates:
            more = min(reach - counts[i], max(1, remaining * loads[i] // pool), surplus)
            counts[i] = counts[i] + more
            surplus = surplus - more
    return np.array([reach] + counts)


def uneven(own_key, count, total, reach, lean):
    if count == 2:
        one = jax.random.randint(own_key, (), max(1, total - reach), min(reach, total - 1) + 1)
        return jnp.stack([one, total - one])
    sizes = jnp.asarray(split_up(count, total, reach, lean), jnp.int32)
    twos = (count - 1) // 2
    giver, receiver = sizes[1:1 + 2 * twos:2], sizes[2:2 + 2 * twos:2]
    margin = jnp.minimum(giver - 1, reach - receiver)
    moved = jax.random.randint(jax.random.fold_in(own_key, 1), (twos,), 0, 1 << 20) % (margin + 1)
    sizes = sizes.at[1:1 + 2 * twos:2].set(giver - moved).at[2:2 + 2 * twos:2].set(receiver + moved)
    return sizes[jax.random.permutation(jax.random.fold_in(own_key, 2), count)]


def bell_draw(rng, extent, spread, reach, shards=(), held_as=jnp.bfloat16):
    drawn = spread * jax.random.normal(rng, extent, jnp.float32)
    if shards:
        drawn = drawn * levels(rng, extent, shards, -0.22, 0.18)
    return jnp.clip(drawn, -reach, reach).astype(held_as)


def setup_inputs(seed: int = 0, part: int = 0) -> dict:
    key_list = jax.random.split(jax.random.key(seed), 9)
    part_splits = jax.random.split(jax.random.fold_in(key_list[8], part), 9)
    return {
        "queries": draw_queries(jax.random.fold_in(jax.random.fold_in(key_list[8], part), 71), part),
        "keys": draw_keys(jax.random.fold_in(jax.random.fold_in(key_list[8], part), 71), part),
        "values": bell_draw(part_splits[2], (TOKENS, D), 1.0, 6.0, ((0, 16),)),
        "out_weight": bell_draw(key_list[3], (D, D), D ** -0.5, 0.1875, ((0, 16),)),
        "grad_output": bell_draw(part_splits[4], (TOKENS, D), 1.0, 6.0, ((0, 16),)),
        "complex_id": jnp.searchsorted(jnp.cumsum(uneven(part_splits[5], N_CTX // 4, TOKENS, 8 * TOK_DEV, 0)), jnp.arange(TOKENS), side="right").astype(jnp.int32),
        "contacts": draw_contacts(jax.random.fold_in(jax.random.fold_in(key_list[8], part), 71), part),
        "contact_count": draw_contact_count(jax.random.fold_in(jax.random.fold_in(key_list[8], part), 71), part),
    }


def block_pass(query, block_keys, block_values, grad_block, allowed):
    rows, width = query.shape
    head_dim = width // HEADS
    scale = 1.0 / math.sqrt(head_dim)
    query_heads = query.astype(jnp.float32).reshape(rows, HEADS, head_dim)
    key_heads = block_keys.astype(jnp.float32).reshape(-1, HEADS, head_dim)
    value_heads = block_values.astype(jnp.float32).reshape(-1, HEADS, head_dim)
    grad_heads = grad_block.astype(jnp.float32).reshape(rows, HEADS, head_dim)
    similarity_logits = jnp.einsum('qhd,khd->hqk', query_heads, key_heads) * scale
    masked = jnp.where(allowed[None], similarity_logits, jnp.float32(-1e+30))
    top = lax.optimization_barrier(jnp.max(masked, axis=2, keepdims=True))
    total = lax.optimization_barrier(jnp.sum(jnp.where(allowed[None], jnp.exp(masked - top), jnp.float32(0.0)), axis=2, keepdims=True))
    log_total = top + jnp.log(total)
    probs = jnp.where(allowed[None], jnp.exp(masked - log_total), jnp.float32(0.0))
    probs_low = lax.optimization_barrier(probs.astype(jnp.bfloat16)).astype(jnp.float32)
    attended = jnp.einsum('hqk,khd->qhd', probs_low, value_heads).astype(jnp.bfloat16)
    attended_wide = lax.optimization_barrier(attended).astype(jnp.float32)
    row_dot = jnp.einsum('qhd,qhd->hq', grad_heads, attended_wide)[..., None]
    grad_probs = jnp.einsum('qhd,khd->hqk', grad_heads, value_heads)
    grad_scores = lax.optimization_barrier((probs * (grad_probs - row_dot)).astype(jnp.bfloat16)).astype(jnp.float32)
    grad_query = (jnp.einsum('hqk,khd->qhd', grad_scores, key_heads) * scale).reshape(rows, width)
    grad_key = (jnp.einsum('hqk,qhd->khd', grad_scores, query_heads) * scale).reshape(-1, width)
    grad_value = jnp.einsum('hqk,qhd->khd', probs_low, grad_heads).reshape(-1, width)
    return (attended.reshape(rows, width), grad_query.astype(jnp.bfloat16), grad_key, grad_value)

def reference(queries, keys, values, out_weight, grad_output, complex_id, contacts, contact_count):
    tokens, width = queries.shape
    nblocks, listed = contacts.shape
    block = tokens // nblocks
    grad_input = jnp.dot(grad_output, out_weight.T, preferred_element_type=jnp.float32).astype(jnp.bfloat16)
    query_blocks = queries.reshape(nblocks, block, width)
    key_blocks = keys.reshape(nblocks, block, width)
    value_blocks = values.reshape(nblocks, block, width)
    grad_blocks = grad_input.reshape(nblocks, block, width)
    id_blocks = complex_id.reshape(nblocks, block)
    slot_live = jnp.arange(listed, dtype=jnp.int32)[None, :] < contact_count[:, None]

    def step(carry, index):
        key_grads, value_grads = carry
        chosen = contacts[index]
        gathered_keys = key_blocks[chosen].reshape(listed * block, width)
        gathered_values = value_blocks[chosen].reshape(listed * block, width)
        live = jnp.repeat(slot_live[index], block)
        allowed = (id_blocks[index][:, None] == id_blocks[chosen].reshape(-1)[None, :]) & live[None, :]
        attended, grad_query, grad_key, grad_value = block_pass(query_blocks[index], gathered_keys, gathered_values, grad_blocks[index], allowed)
        key_grads = key_grads.at[chosen].add(grad_key.reshape(listed, block, width))
        value_grads = value_grads.at[chosen].add(grad_value.reshape(listed, block, width))
        return ((key_grads, value_grads), (attended, grad_query))
    start = jnp.zeros((nblocks, block, width), jnp.float32)
    (key_grads, value_grads), (attended, grad_query) = lax.scan(step, (start, start), jnp.arange(nblocks, dtype=jnp.int32))
    attended = attended.reshape(tokens, width)
    mixed = jnp.dot(attended, out_weight, preferred_element_type=jnp.float32).astype(jnp.bfloat16)
    grad_weight = jnp.dot(attended.T, grad_output, preferred_element_type=jnp.float32) * jnp.float32(1.0 / math.sqrt(tokens))
    return (mixed, grad_query.reshape(tokens, width), key_grads.reshape(tokens, width).astype(jnp.bfloat16), value_grads.reshape(tokens, width).astype(jnp.bfloat16), grad_weight)
```

```python
import functools
import math

import jax
import jax.numpy as jnp
from jax import lax
from jax.experimental import pallas as pl
from jax.experimental.pallas import tpu as pltpu
from jax.sharding import PartitionSpec as P

HEADS = 16
REACH_DEV = 2
LANES = 128
AHEAD_KV = 3
AHEAD_W = 3


def layer_kernel(
    n, blocks, listed, block, head_dim, tokens,
    contacts, count, ids, q_hbm, k_hbm, v_hbm, w_hbm, g_hbm,
    mixed_hbm, dq_hbm, dk_hbm, dv_hbm, gw_hbm,
    q_v, k_v, v_v, g_v, wbuf, land, idt, bias, kwin, vwin, kg, vg, dks, dvs,
    own, far, got_f, got_c, got_z, got_y, put_z, put_y, outg, dqb, att_v, mix_v,
    gwp, core_got, gsum, rsbuf, ysend, ybuf, gfin, gwout, inv,
    local_sem, y_s, y_r, c_s, c_r, z_s, z_r, o_s, o_r,
    wy_s, w_s, w_r, wc_s, wc_r, ret_s, ret_r, gc_s, gc_r, gz_s, gz_r, gy_s, gy_r,
    out_sem, fin_sem,
):
    f32, bf16 = jnp.float32, jnp.bfloat16
    rows = blocks * block
    width = q_hbm.shape[1]
    pairs = width // LANES
    wrows = w_hbm.shape[0]
    nz = n // 4
    chips = LANES // (2 * wrows)
    reach = REACH_DEV * blocks
    windows = (2 * REACH_DEV + 1) * blocks
    scale = 1.0 / math.sqrt(head_dim)

    me = lax.axis_index("ctx")
    core, y, z = lax.rem(me, 2), lax.rem(me // 2, 2), me // 4
    ypeer, cpeer = me + 2 - 4 * y, me + 1 - 2 * core
    ahead, behind = me + 4 - 8 * y, me - 4 + 8 * y
    has_ahead = (ahead >= 0) & (ahead < n)
    has_behind = (behind >= 0) & (behind < n)

    def column(k):
        other = lax.rem(z + k, nz)
        return other, other * 4 + y * 2 + core

    def remote(src, dst, send, recv, device):
        return pltpu.make_async_remote_copy(
            src_ref=src, dst_ref=dst, send_sem=send, recv_sem=recv,
            device_id={"ctx": device}, device_id_type=pl.DeviceIdType.MESH,
        )

    def over(start, stop, body):
        lax.fori_loop(start, stop, lambda i, c: (body(i), c)[1], 0)

    def lanes(p):
        return pl.ds(pl.multiple_of(p * LANES, LANES), LANES)

    def shard(d):
        return pl.ds(pl.multiple_of(d * wrows, wrows), wrows)

    def kv_y(a, p):
        return remote(
            (k_hbm, v_hbm)[a].at[:, lanes(p)], land.at[p, 3 * y, a], y_s.at[a, p], y_r.at[a, p], ypeer
        )

    def kv_c(a, p):
        return remote(
            (k_hbm, v_hbm)[a].at[:, lanes(p)], land.at[p, 1 + core, a], c_s.at[a, p], c_r.at[a, p], cpeer
        )

    def kv_z(p):
        return remote(land.at[p, 3 - 3 * y], land.at[p, 3 * y], z_s.at[p], z_r.at[p], ahead)

    def kv_on(p):
        return remote(land.at[p, 3 - 3 * core], land.at[p, 2 - core], o_s.at[p], o_r.at[p], cpeer)

    on_sent = (y == core) | has_behind
    on_got = (y != core) | has_behind

    def kv_start(p):
        for a in range(2):
            kv_y(a, p).start()
        for a in range(2):
            kv_c(a, p).start()

    def kv_first(p):
        for a in range(2):
            kv_y(a, p).wait_recv()
        pl.when(has_ahead)(lambda: kv_z(p).start())
        pl.when(y == core)(lambda: kv_on(p).start())

    def kv_second(p):
        @pl.when(has_behind)
        def _():
            kv_z(p).wait_recv()
            pl.when(y != core)(lambda: kv_on(p).start())

    def kv_wait(p):
        for a in range(2):
            kv_c(a, p).wait_recv()
        pl.when(on_got)(lambda: kv_on(p).wait_recv())

    mychip, ychip = me // 2, me // 2 + 1 - 2 * y

    def w_y():
        return remote(w_hbm, wbuf.at[shard(me)], wy_s, w_r.at[mychip], ypeer)

    def w_in(chip):
        d = shard(2 * chip + core)
        return remote(wbuf.at[d], wbuf.at[d], wy_s, w_r.at[chip], ypeer)

    def w_z(mine, k):
        _, device = column(k)
        if mine:
            return remote(w_hbm, wbuf.at[shard(me)], w_s.at[0, k], w_r.at[mychip], device)
        d = shard(2 * ychip + core)
        return remote(wbuf.at[d], wbuf.at[d], w_s.at[1, k], w_r.at[ychip], device)

    def w_c(chip):
        d = shard(2 * chip + core)
        return remote(wbuf.at[d], wbuf.at[d], wc_s.at[chip], wc_r.at[chip], cpeer)

    def w_send(p):
        for i in range(chips):
            chip = p * chips + i

            @pl.when(chip == mychip)
            def _():
                over(1, nz, lambda k: w_z(True, k).start())

            @pl.when(chip == ychip)
            def _():
                w_in(ychip).wait_recv()
                over(1, nz, lambda k: w_z(False, k).start())

    def w_forward(p):
        for i in range(chips):
            chip = p * chips + i
            pl.when((chip != mychip) & (chip != ychip))(lambda chip=chip: w_in(chip).wait_recv())
            w_c(chip).start()

    def w_wait(p):
        for i in range(chips):
            w_c(p * chips + i).wait_recv()

    def back(p):
        return remote(far.at[p, 1 + core], got_f.at[p], ret_s.at[0, p], ret_r.at[0, p], cpeer)

    def across(p):
        return remote(far.at[p, 2 - core], got_c.at[p], ret_s.at[1, p], ret_r.at[1, p], cpeer)

    def ret_z(p):
        return remote(put_z.at[p], got_z.at[p], ret_s.at[2, p], ret_r.at[2, p], behind)

    def ret_y(p):
        return remote(put_y.at[p], got_y.at[p], ret_s.at[3, p], ret_r.at[3, p], ypeer)

    sent_back = (y != core) | has_behind
    got_back = (y == core) | has_behind

    def ret_one(p):
        pl.when(sent_back)(lambda: back(p).start())
        across(p).start()

    def ret_two(p):
        pl.when(got_back)(lambda: back(p).wait_recv())
        value = far[p, 3 * y].astype(f32)
        put_z[p] = (value + jnp.where(y != core, got_f[p].astype(f32), 0.0)).astype(bf16)
        pl.when(has_behind)(lambda: ret_z(p).start())

    def ret_three(p):
        pl.when(has_ahead)(lambda: ret_z(p).wait_recv())
        value = far[p, 3 - 3 * y].astype(f32)
        value = value + jnp.where(has_ahead, got_z[p].astype(f32), 0.0)
        value = value + jnp.where(y == core, got_f[p].astype(f32), 0.0)
        put_y[p] = value.astype(bf16)
        ret_y(p).start()

    def out_copy(a, p):
        src = dqb.at[p] if a == 2 else outg.at[p, a]
        return pltpu.make_async_copy(src, (dk_hbm, dv_hbm, dq_hbm)[a].at[:, lanes(p)], out_sem.at[a, p])

    def ret_four(p):
        across(p).wait_recv()
        ret_y(p).wait_recv()
        outg[p] = (own[p] + got_c[p].astype(f32) + got_y[p].astype(f32)).astype(bf16)
        for a in range(2):
            out_copy(a, p).start()

    def gw_c(chip):
        return remote(
            gwp.at[shard(2 * chip + 1 - core)], core_got.at[chip], gc_s.at[chip], gc_r.at[chip], cpeer
        )

    def gw_z(chip):
        zc, yc = chip // 2, lax.rem(chip, 2)
        return remote(gsum.at[chip], rsbuf.at[yc, z], gz_s.at[chip], gz_r.at[yc, z], zc * 4 + y * 2 + core)

    def gw_in(yc, other):
        return remote(gsum.at[0], rsbuf.at[yc, other], gz_s.at[0], gz_r.at[yc, other], ypeer)

    def gw_y():
        return remote(ysend, ybuf, gy_s, gy_r, ypeer)

    def gw_one(p):
        for i in range(chips):
            gw_c(p * chips + i).start()

    def gw_two(p):
        for i in range(chips):
            chip = p * chips + i
            zc, yc = chip // 2, lax.rem(chip, 2)
            gw_c(chip).wait_recv()
            value = gwp[shard(2 * chip + core), :].astype(f32) + core_got[chip].astype(f32)
            gsum[chip] = value.astype(bf16)
            pl.when(zc != z)(lambda chip=chip: gw_z(chip).start())

            @pl.when(zc == z)
            def _(value=value, yc=yc):
                rsbuf[yc, z] = value.astype(bf16)

    def gw_three(p):
        for i in range(chips):
            chip = p * chips + i
            yc = lax.rem(chip, 2)

            @pl.when(chip // 2 == z)
            def _(yc=yc):
                over(1, nz, lambda k: gw_in(yc, column(k)[0]).wait_recv())
                value = rsbuf[yc, 0].astype(f32)
                for other in range(1, nz):
                    value = value + rsbuf[yc, other].astype(f32)

                @pl.when(yc == y)
                def _():
                    gfin[...] = value

                @pl.when(yc != y)
                def _():
                    ysend[...] = value.astype(bf16)
                    gw_y().start()

    barrier = pltpu.get_barrier_semaphore()

    def hello(device):
        pl.semaphore_signal(barrier, inc=1, device_id={"ctx": device}, device_id_type=pl.DeviceIdType.MESH)

    hello(ypeer)
    hello(cpeer)
    over(1, nz, lambda k: hello(column(k)[1]))
    pl.semaphore_wait(barrier, nz + 1)

    w_y().start()
    kv_start(0)
    loads = [
        pltpu.make_async_copy(w_hbm, wbuf.at[shard(me)], local_sem.at[0]),
        pltpu.make_async_copy(g_hbm, g_v, local_sem.at[1]),
        pltpu.make_async_copy(q_hbm, q_v, local_sem.at[2]),
        pltpu.make_async_copy(k_hbm, k_v, local_sem.at[3]),
        pltpu.make_async_copy(v_hbm, v_v, local_sem.at[4]),
    ]
    for copy in loads:
        copy.start()
    for p in range(1, AHEAD_KV):
        kv_start(p)
    for p in range(AHEAD_W):
        w_send(p)

    first = me * blocks - reach
    total_blocks = ids.shape[0]
    for w in range(windows):
        at = jnp.clip(first + w, 0, total_blocks - 1)
        row = ids[pl.ds(at, 1), :].astype(f32)
        idt[w] = jnp.broadcast_to(row, (block, block)).T
    local = [[jnp.clip(contacts[b, j] - first, 0, windows - 1) for j in range(listed)] for b in range(blocks)]
    for b in range(blocks):
        mine = ids[pl.ds(me * blocks + b, 1), :].astype(f32)
        for j in range(listed):
            same = idt[local[b][j]] == mine
            alive = jnp.full((block, LANES), count[b], jnp.int32) > j
            bias[pl.ds((b * listed + j) * block, block), :] = jnp.where(same & alive, 0.0, -jnp.inf)
        for w in range(2 * reach + 1):
            slot = jnp.int32(blocks * listed)
            for j in range(listed):
                slot = jnp.where(local[b][j] == w + b, b * listed + j, slot)
            inv[b, w] = slot
    for ref in (dks, dvs):
        ref[blocks * listed] = jnp.zeros((block, LANES), f32)
    for copy in loads:
        copy.wait()

    lane = lax.broadcasted_iota(jnp.int32, (block, LANES), 1) < head_dim
    sub = lax.broadcasted_iota(jnp.int32, (LANES, block), 0) < head_dim
    last_dim = (((1,), (1,)), ((), ()))
    first_dim = (((0,), (0,)), ((), ()))

    def two(x):
        zero = jnp.zeros_like(x)
        return jnp.concatenate([jnp.where(lane, x, zero), jnp.where(lane, zero, x)], axis=0).astype(bf16)

    def attend(p):
        cols = lanes(p)
        grad_all = lax.dot_general(
            g_v[...], wbuf[cols, :], last_dim, preferred_element_type=f32
        ).astype(bf16)
        for i, piece in enumerate((0, 1, None, 2, 3)):
            span = pl.ds(i * blocks, blocks)
            kwin[span] = (k_v[:, cols] if piece is None else land[p, piece, 0]).reshape(blocks, block, LANES)
            vwin[span] = (v_v[:, cols] if piece is None else land[p, piece, 1]).reshape(blocks, block, LANES)
        for b in range(blocks):
            here = pl.ds(b * block, block)
            for j in range(listed):
                at = jnp.clip(contacts[b, j] - first, 0, windows - 1)
                kg[pl.ds(j * block, block), :] = kwin[at]
                vg[pl.ds(j * block, block), :] = vwin[at]
            grad = grad_all[b * block : (b + 1) * block].astype(f32)
            q2 = two(q_v[here, cols].astype(f32) * scale)
            d2 = two(grad)
            s = lax.dot_general(kg[...], q2, last_dim, preferred_element_type=f32)
            mask = bias[pl.ds(b * listed * block, listed * block), :]
            s = s + jnp.concatenate([mask, mask], axis=1)
            top = jnp.max(s, axis=0, keepdims=True)
            e = jnp.exp(s - top)
            probs = e * (1.0 / jnp.sum(e, axis=0, keepdims=True))
            low = probs.astype(bf16)
            ot = lax.dot_general(vg[...], low, first_dim, preferred_element_type=f32)
            att = jnp.where(sub, ot[:, :block], ot[:, block:]).astype(bf16).astype(f32)
            att_v[here, cols] = att.T.astype(bf16)
            prod = grad.T * att
            row_dot = jnp.concatenate(
                [jnp.sum(prod[:head_dim], axis=0, keepdims=True), jnp.sum(prod[head_dim:], axis=0, keepdims=True)],
                axis=1,
            )
            dp = lax.dot_general(vg[...], d2, last_dim, preferred_element_type=f32)
            ds = (probs * (dp - row_dot)).astype(bf16)
            dqt = lax.dot_general(kg[...], ds, first_dim, preferred_element_type=f32)
            dq = jnp.where(sub, dqt[:, :block], dqt[:, block:]) * scale
            dqb[p, here, :] = dq.T.astype(bf16)
            part = pl.ds(b * listed, listed)
            dks[part] = jnp.dot(ds, q2, preferred_element_type=f32).reshape(listed, block, LANES)
            dvs[part] = jnp.dot(low, d2, preferred_element_type=f32).reshape(listed, block, LANES)
        out_copy(2, p).start()
        for a, slots in enumerate((dks, dvs)):
            for w in range(windows):
                value = None
                for b in range(blocks):
                    if 0 <= w - b <= 2 * reach:
                        term = slots[inv[b, w - b]]
                        value = term if value is None else value + term
                piece, part = w // blocks, pl.ds((w % blocks) * block, block)
                if piece == REACH_DEV:
                    own[p, a, part, :] = value
                else:
                    far[p, piece - (piece > REACH_DEV), a, part, :] = value.astype(bf16)
        ret_one(p)
        gwp[cols, :] = lax.dot_general(
            att_v[:, cols], g_v[...], first_dim, preferred_element_type=f32
        ).astype(bf16)
        gw_one(p)

    kv_first(0)
    kv_first(1)
    kv_second(0)
    w_forward(0)

    def step(p):
        pl.when(p + AHEAD_KV < pairs)(lambda: kv_start(p + AHEAD_KV))
        pl.when(p + 2 < pairs)(lambda: kv_first(p + 2))

        @pl.when(p + 1 < pairs)
        def _():
            kv_second(p + 1)
            w_forward(p + 1)

        pl.when(p + AHEAD_W < pairs)(lambda: w_send(p + AHEAD_W))

        @pl.when(p < pairs)
        def _():
            kv_wait(p)
            w_wait(p)
            attend(p)

        @pl.when((p >= 1) & (p <= pairs))
        def _():
            ret_two(p - 1)
            gw_two(p - 1)

        pl.when((p >= 2) & (p <= pairs + 1))(lambda: ret_three(p - 2))

        @pl.when(p == pairs)
        def _():
            mix_v[...] = jnp.dot(att_v[...], wbuf[...], preferred_element_type=f32).astype(bf16)
            pltpu.make_async_copy(mix_v, mixed_hbm, fin_sem.at[0]).start()

        @pl.when(p >= 3)
        def _():
            ret_four(p - 3)
            gw_three(p - 3)

    over(0, pairs + 3, step)

    gw_y().wait_recv()
    gwout[...] = (gfin[...] + ybuf[...].astype(f32)) * jnp.float32(1.0 / math.sqrt(tokens))
    pltpu.make_async_copy(gwout, gw_hbm, fin_sem.at[1]).start()

    w_y().wait_send()
    for mine in (True, False):
        over(1, nz, lambda k: w_z(mine, k).wait_send())

    def sent(p):
        for a in range(2):
            kv_y(a, p).wait_send()
            kv_c(a, p).wait_send()
        pl.when(has_ahead)(lambda: kv_z(p).wait_send())
        pl.when(on_sent)(lambda: kv_on(p).wait_send())
        pl.when(sent_back)(lambda: back(p).wait_send())
        across(p).wait_send()
        pl.when(has_behind)(lambda: ret_z(p).wait_send())
        ret_y(p).wait_send()
        for a in range(3):
            out_copy(a, p).wait()
        for i in range(chips):
            chip = p * chips + i
            w_c(chip).wait_send()
            gw_c(chip).wait_send()
            pl.when(chip // 2 != z)(lambda chip=chip: gw_z(chip).wait_send())

    over(0, pairs, sent)
    gw_y().wait_send()
    pltpu.make_async_copy(mix_v, mixed_hbm, fin_sem.at[0]).wait()
    pltpu.make_async_copy(gwout, gw_hbm, fin_sem.at[1]).wait()


def layer(contacts, count, ids, queries, keys, values, weight, grad_output):
    n = lax.axis_size("ctx")
    rows, width = queries.shape
    blocks, listed = contacts.shape
    block = rows // blocks
    wrows = weight.shape[0]
    pairs, nz = width // LANES, n // 4
    window = (2 * REACH_DEV + 1) * blocks
    f32, bf16 = jnp.float32, jnp.bfloat16
    vmem, dma = pltpu.VMEM, pltpu.SemaphoreType.DMA
    smem = pl.BlockSpec(memory_space=pltpu.SMEM)
    hbm = pl.BlockSpec(memory_space=pl.ANY)
    slots = blocks * listed + 1
    flat, both = (rows, width), (pairs, 2, rows, LANES)
    return pl.pallas_call(
        functools.partial(layer_kernel, n, blocks, listed, block, width // HEADS, rows * n),
        in_specs=[smem, smem, pl.BlockSpec(memory_space=pltpu.VMEM)] + [hbm] * 5,
        out_specs=[hbm] * 5,
        out_shape=[jax.ShapeDtypeStruct(flat, bf16)] * 4 + [jax.ShapeDtypeStruct((wrows, width), f32)],
        scratch_shapes=[vmem(flat, bf16)] * 4
        + [
            vmem((width, width), bf16),
            vmem((pairs, 2 * REACH_DEV, 2, rows, LANES), bf16),
            vmem((window, block, block), f32),
            vmem((blocks * listed * block, LANES), f32),
            vmem((window, block, LANES), bf16),
            vmem((window, block, LANES), bf16),
            vmem((listed * block, LANES), bf16),
            vmem((listed * block, LANES), bf16),
            vmem((slots, block, LANES), f32),
            vmem((slots, block, LANES), f32),
            vmem(both, f32),
            vmem((pairs, 2 * REACH_DEV, 2, rows, LANES), bf16),
        ]
        + [vmem(both, bf16)] * 7
        + [
            vmem((pairs, rows, LANES), bf16),
            vmem(flat, bf16),
            vmem(flat, bf16),
            vmem((width, width), bf16),
            vmem((n // 2, wrows, width), bf16),
            vmem((n // 2, wrows, width), bf16),
            vmem((2, nz, wrows, width), bf16),
            vmem((wrows, width), bf16),
            vmem((wrows, width), bf16),
            vmem((wrows, width), f32),
            vmem((wrows, width), f32),
            pltpu.SMEM((blocks, 2 * REACH_DEV * blocks + 1), jnp.int32),
            dma((5,)),
        ]
        + [dma((2, pairs))] * 4
        + [dma((pairs,))] * 4
        + [dma, dma((2, nz))]
        + [dma((n // 2,))] * 3
        + [dma((4, pairs))] * 2
        + [dma((n // 2,))] * 3
        + [dma((2, nz)), dma, dma, dma((3, pairs)), dma((2,))],
        compiler_params=pltpu.CompilerParams(
            collective_id=0, has_side_effects=True, vmem_limit_bytes=60 * 1024 * 1024
        ),
        name="contact_layer",
    )(contacts, count, ids, queries, keys, values, weight, grad_output)


def shards(queries, keys, values, out_weight, grad_output, complex_id, contacts, contact_count):
    block = queries.shape[0] // contacts.shape[0]
    return layer(
        contacts, contact_count, complex_id.reshape(-1, block), queries, keys, values, out_weight, grad_output
    )


def solution(mesh):
    split = P(("groups", "ctx"), None)
    return jax.shard_map(
        shards,
        mesh=mesh,
        in_specs=(split, split, split, P("ctx", None), split, P("groups"), split, P(("groups", "ctx"))),
        out_specs=(split,) * 5,
        check_vma=False,
    )
```

```python
import functools
import math

import jax
import jax.numpy as jnp
from jax import lax
from jax.experimental import pallas as pl
from jax.experimental.pallas import tpu as pltpu
from jax.sharding import PartitionSpec as P

HEADS = 16
REACH_DEV = 2
LANES = 128
AHEAD_KV = 3
LEAD = 4


def layer_kernel(
    n, blocks, listed, block, head_dim, tokens,
    contacts, count, ids, q_hbm, k_hbm, v_hbm, w_hbm, g_hbm,
    mixed_hbm, dq_hbm, dk_hbm, dv_hbm, gw_hbm,
    q_v, k_v, v_v, g_v, wbuf, land, idt, bias, kwin, vwin, kg, vg, dks, dvs,
    own, far, got_f, got_c, got_z, got_y, put_z, put_y, outg, dqb, att_v, mix_v,
    gwp, core_got, gsum, gin, ysend, ybuf, gfin, gwout, inv,
    local_sem, y_s, y_r, c_s, c_r, z_s, z_r, o_s, o_r,
    wy_s, w_s, w_r, wc_s, wc_r, ret_s, ret_r, gc_s, gc_r, gz_s, gz_r, gy_s, gy_r,
    out_sem, fin_sem,
):
    f32, bf16 = jnp.float32, jnp.bfloat16
    rows = blocks * block
    width = q_hbm.shape[1]
    pairs = width // LANES
    wrows = w_hbm.shape[0]
    nz = n // 4
    chips = LANES // (2 * wrows)
    reach = REACH_DEV * blocks
    windows = (2 * REACH_DEV + 1) * blocks
    scale = 1.0 / math.sqrt(head_dim)

    me = lax.axis_index("ctx")
    core, y, z = lax.rem(me, 2), lax.rem(me // 2, 2), me // 4
    ypeer, cpeer = me + 2 - 4 * y, me + 1 - 2 * core
    ahead, behind = me + 4 - 8 * y, me - 4 + 8 * y
    has_ahead = (ahead >= 0) & (ahead < n)
    has_behind = (behind >= 0) & (behind < n)

    def remote(src, dst, send, recv, device):
        return pltpu.make_async_remote_copy(
            src_ref=src, dst_ref=dst, send_sem=send, recv_sem=recv,
            device_id={"ctx": device}, device_id_type=pl.DeviceIdType.MESH,
        )

    def over(start, stop, body):
        lax.fori_loop(start, stop, lambda i, c: (body(i), c)[1], 0)

    def turn(p):
        return p + 2 - 4 * lax.rem(p // 2, 2)

    def lanes(p):
        return pl.ds(pl.multiple_of(turn(p) * LANES, LANES), LANES)

    def shard(d):
        return pl.ds(pl.multiple_of(d * wrows, wrows), wrows)

    def kv_y(a, p):
        return remote(
            (k_hbm, v_hbm)[a].at[:, lanes(p)], land.at[p, 3 * y, a], y_s.at[a, p], y_r.at[a, p], ypeer
        )

    def kv_c(a, p):
        return remote(
            (k_hbm, v_hbm)[a].at[:, lanes(p)], land.at[p, 1 + core, a], c_s.at[a, p], c_r.at[a, p], cpeer
        )

    def kv_z(p):
        return remote(land.at[p, 3 - 3 * y], land.at[p, 3 * y], z_s.at[p], z_r.at[p], ahead)

    def kv_on(p):
        return remote(land.at[p, 3 - 3 * core], land.at[p, 2 - core], o_s.at[p], o_r.at[p], cpeer)

    on_sent = (y == core) | has_behind
    on_got = (y != core) | has_behind

    def kv_start(p):
        for a in range(2):
            kv_y(a, p).start()
        for a in range(2):
            kv_c(a, p).start()

    def kv_first(p):
        for a in range(2):
            kv_y(a, p).wait_recv()
        pl.when(has_ahead)(lambda: kv_z(p).start())
        pl.when(y == core)(lambda: kv_on(p).start())

    def kv_second(p):
        @pl.when(has_behind)
        def _():
            kv_z(p).wait_recv()
            pl.when(y != core)(lambda: kv_on(p).start())

    def kv_wait(p):
        for a in range(2):
            kv_c(a, p).wait_recv()
        pl.when(on_got)(lambda: kv_on(p).wait_recv())

    mychip = me // 2

    def w_y():
        return remote(w_hbm, wbuf.at[shard(me)], wy_s, w_r.at[mychip], ypeer)

    def w_in(chip):
        d = shard(2 * chip + core)
        return remote(wbuf.at[d], wbuf.at[d], wy_s, w_r.at[chip], ypeer)

    def w_z(chip, up):
        d = shard(2 * chip + core)
        return remote(wbuf.at[d], wbuf.at[d], w_s.at[up, chip], w_r.at[chip], me - 4 + 8 * up)

    def w_c(chip):
        d = shard(2 * chip + core)
        return remote(wbuf.at[d], wbuf.at[d], wc_s.at[chip], wc_r.at[chip], cpeer)

    def w_goes(chip):
        zc = chip // 2
        return (z >= zc) & (z + 1 < nz), (z <= zc) & (z > 0)

    def w_hop(p, lead):
        for i in range(chips):
            chip = turn(p) * chips + i
            far_off = jnp.abs(z - chip // 2)

            @pl.when(jnp.maximum(1, LEAD - far_off) == lead)
            def _(chip=chip):
                up, down = w_goes(chip)
                pl.when(chip != mychip)(lambda: w_in(chip).wait_recv())
                pl.when(up)(lambda: w_z(chip, 1).start())
                pl.when(down)(lambda: w_z(chip, 0).start())
                w_c(chip).start()

    def w_wait(p):
        for i in range(chips):
            w_c(turn(p) * chips + i).wait_recv()

    def back(p):
        return remote(far.at[p, 1 + core], got_f.at[p], ret_s.at[0, p], ret_r.at[0, p], cpeer)

    def across(p):
        return remote(far.at[p, 2 - core], got_c.at[p], ret_s.at[1, p], ret_r.at[1, p], cpeer)

    def ret_z(p):
        return remote(put_z.at[p], got_z.at[p], ret_s.at[2, p], ret_r.at[2, p], behind)

    def ret_y(p):
        return remote(put_y.at[p], got_y.at[p], ret_s.at[3, p], ret_r.at[3, p], ypeer)

    sent_back = (y != core) | has_behind
    got_back = (y == core) | has_behind

    def ret_one(p):
        pl.when(sent_back)(lambda: back(p).start())
        across(p).start()

    def ret_two(p):
        pl.when(got_back)(lambda: back(p).wait_recv())
        value = far[p, 3 * y].astype(f32)
        put_z[p] = (value + jnp.where(y != core, got_f[p].astype(f32), 0.0)).astype(bf16)
        pl.when(has_behind)(lambda: ret_z(p).start())

    def ret_three(p):
        pl.when(has_ahead)(lambda: ret_z(p).wait_recv())
        value = far[p, 3 - 3 * y].astype(f32)
        value = value + jnp.where(has_ahead, got_z[p].astype(f32), 0.0)
        value = value + jnp.where(y == core, got_f[p].astype(f32), 0.0)
        put_y[p] = value.astype(bf16)
        ret_y(p).start()

    def out_copy(a, p):
        src = dqb.at[p] if a == 2 else outg.at[p, a]
        return pltpu.make_async_copy(src, (dk_hbm, dv_hbm, dq_hbm)[a].at[:, lanes(p)], out_sem.at[a, p])

    def ret_four(p):
        across(p).wait_recv()
        ret_y(p).wait_recv()
        outg[p] = (own[p] + got_c[p].astype(f32) + got_y[p].astype(f32)).astype(bf16)
        for a in range(2):
            out_copy(a, p).start()

    def gw_c(chip):
        return remote(
            gwp.at[shard(2 * chip + 1 - core)], core_got.at[chip], gc_s.at[chip], gc_r.at[chip], cpeer
        )

    def gw_z(chip):
        side = (z > chip // 2).astype(jnp.int32)
        return remote(
            gsum.at[chip], gin.at[side, chip], gz_s.at[chip], gz_r.at[side, chip], me + 4 - 8 * side
        )

    def gw_in(chip, side):
        return remote(gsum.at[chip], gin.at[side, chip], gz_s.at[chip], gz_r.at[side, chip], ypeer)

    def gw_y():
        return remote(ysend, ybuf, gy_s, gy_r, ypeer)

    def gw_one(p):
        for i in range(chips):
            gw_c(turn(p) * chips + i).start()

    def gw_two(p):
        for i in range(chips):
            chip = turn(p) * chips + i
            zc = chip // 2
            gw_c(chip).wait_recv()
            value = gwp[shard(2 * chip + core), :].astype(f32) + core_got[chip].astype(f32)
            gsum[chip] = value.astype(bf16)
            ends = ((z == 0) & (zc > 0)) | ((z == nz - 1) & (zc < nz - 1))
            pl.when(ends)(lambda chip=chip: gw_z(chip).start())

    def gw_hop(p, lag):
        for i in range(chips):
            chip = turn(p) * chips + i
            zc = chip // 2
            stage = jnp.where(z < zc, z, nz - 1 - z)

            @pl.when((z != zc) & (stage > 0) & (jnp.minimum(stage + 1, LEAD - 1) == lag))
            def _(chip=chip, zc=zc):
                side = (z > zc).astype(jnp.int32)
                gw_in(chip, side).wait_recv()
                gsum[chip] = (gsum[chip].astype(f32) + gin[side, chip].astype(f32)).astype(bf16)
                gw_z(chip).start()

            @pl.when((z == zc) & (jnp.minimum(jnp.maximum(zc, nz - 1 - zc) + 1, LEAD) == lag))
            def _(chip=chip):
                yc = lax.rem(chip, 2)
                pl.when(z > 0)(lambda: gw_in(chip, 0).wait_recv())
                pl.when(z < nz - 1)(lambda: gw_in(chip, 1).wait_recv())
                value = gsum[chip].astype(f32)
                value = value + jnp.where(z > 0, gin[0, chip].astype(f32), 0.0)
                value = value + jnp.where(z < nz - 1, gin[1, chip].astype(f32), 0.0)

                @pl.when(yc == y)
                def _():
                    gfin[...] = value

                @pl.when(yc != y)
                def _():
                    ysend[...] = value.astype(bf16)
                    gw_y().start()

    barrier = pltpu.get_barrier_semaphore()

    def hello(device):
        pl.semaphore_signal(barrier, inc=1, device_id={"ctx": device}, device_id_type=pl.DeviceIdType.MESH)

    hello(ypeer)
    hello(cpeer)
    pl.when(z > 0)(lambda: hello(me - 4))
    pl.when(z < nz - 1)(lambda: hello(me + 4))
    pl.semaphore_wait(barrier, 2 + (z > 0).astype(jnp.int32) + (z < nz - 1).astype(jnp.int32))

    w_y().start()
    kv_start(0)
    loads = [
        pltpu.make_async_copy(w_hbm, wbuf.at[shard(me)], local_sem.at[0]),
        pltpu.make_async_copy(g_hbm, g_v, local_sem.at[1]),
        pltpu.make_async_copy(q_hbm, q_v, local_sem.at[2]),
        pltpu.make_async_copy(k_hbm, k_v, local_sem.at[3]),
        pltpu.make_async_copy(v_hbm, v_v, local_sem.at[4]),
    ]
    for copy in loads:
        copy.start()
    for p in range(1, AHEAD_KV):
        kv_start(p)
    loads[0].wait()

    first = me * blocks - reach

    def setup():
        total_blocks = ids.shape[0]
        for w in range(windows):
            at = jnp.clip(first + w, 0, total_blocks - 1)
            row = ids[pl.ds(at, 1), :].astype(f32)
            idt[w] = jnp.broadcast_to(row, (block, block)).T
        local = [[jnp.clip(contacts[b, j] - first, 0, windows - 1) for j in range(listed)] for b in range(blocks)]
        for b in range(blocks):
            mine = ids[pl.ds(me * blocks + b, 1), :].astype(f32)
            for j in range(listed):
                same = idt[local[b][j]] == mine
                alive = jnp.full((block, LANES), count[b], jnp.int32) > j
                bias[pl.ds((b * listed + j) * block, block), :] = jnp.where(same & alive, 0.0, -jnp.inf)
            for w in range(2 * reach + 1):
                slot = jnp.int32(blocks * listed)
                for j in range(listed):
                    slot = jnp.where(local[b][j] == w + b, b * listed + j, slot)
                inv[b, w] = slot
        for ref in (dks, dvs):
            ref[blocks * listed] = jnp.zeros((block, LANES), f32)
        for copy in loads[1:]:
            copy.wait()

    lane = lax.broadcasted_iota(jnp.int32, (block, LANES), 1) < head_dim
    sub = lax.broadcasted_iota(jnp.int32, (LANES, block), 0) < head_dim
    last_dim = (((1,), (1,)), ((), ()))
    first_dim = (((0,), (0,)), ((), ()))

    def two(x):
        zero = jnp.zeros_like(x)
        return jnp.concatenate([jnp.where(lane, x, zero), jnp.where(lane, zero, x)], axis=0).astype(bf16)

    def attend(p):
        cols = lanes(p)
        grad_all = lax.dot_general(
            g_v[...], wbuf[cols, :], last_dim, preferred_element_type=f32
        ).astype(bf16)
        for i, piece in enumerate((0, 1, None, 2, 3)):
            span = pl.ds(i * blocks, blocks)
            kwin[span] = (k_v[:, cols] if piece is None else land[p, piece, 0]).reshape(blocks, block, LANES)
            vwin[span] = (v_v[:, cols] if piece is None else land[p, piece, 1]).reshape(blocks, block, LANES)
        for b in range(blocks):
            here = pl.ds(b * block, block)
            for j in range(listed):
                at = jnp.clip(contacts[b, j] - first, 0, windows - 1)
                kg[pl.ds(j * block, block), :] = kwin[at]
                vg[pl.ds(j * block, block), :] = vwin[at]
            grad = grad_all[b * block : (b + 1) * block].astype(f32)
            q2 = two(q_v[here, cols].astype(f32) * scale)
            d2 = two(grad)
            s = lax.dot_general(kg[...], q2, last_dim, preferred_element_type=f32)
            mask = bias[pl.ds(b * listed * block, listed * block), :]
            s = s + jnp.concatenate([mask, mask], axis=1)
            top = jnp.max(s, axis=0, keepdims=True)
            e = jnp.exp(s - top)
            probs = e * (1.0 / jnp.sum(e, axis=0, keepdims=True))
            low = probs.astype(bf16)
            ot = lax.dot_general(vg[...], low, first_dim, preferred_element_type=f32)
            att = jnp.where(sub, ot[:, :block], ot[:, block:]).astype(bf16).astype(f32)
            att_v[here, cols] = att.T.astype(bf16)
            prod = grad.T * att
            row_dot = jnp.concatenate(
                [jnp.sum(prod[:head_dim], axis=0, keepdims=True), jnp.sum(prod[head_dim:], axis=0, keepdims=True)],
                axis=1,
            )
            dp = lax.dot_general(vg[...], d2, last_dim, preferred_element_type=f32)
            ds = (probs * (dp - row_dot)).astype(bf16)
            dqt = lax.dot_general(kg[...], ds, first_dim, preferred_element_type=f32)
            dq = jnp.where(sub, dqt[:, :block], dqt[:, block:]) * scale
            dqb[p, here, :] = dq.T.astype(bf16)
            part = pl.ds(b * listed, listed)
            dks[part] = jnp.dot(ds, q2, preferred_element_type=f32).reshape(listed, block, LANES)
            dvs[part] = jnp.dot(low, d2, preferred_element_type=f32).reshape(listed, block, LANES)
        out_copy(2, p).start()
        for a, slots in enumerate((dks, dvs)):
            for w in range(windows):
                value = None
                for b in range(blocks):
                    if 0 <= w - b <= 2 * reach:
                        term = slots[inv[b, w - b]]
                        value = term if value is None else value + term
                piece, part = w // blocks, pl.ds((w % blocks) * block, block)
                if piece == REACH_DEV:
                    own[p, a, part, :] = value
                else:
                    far[p, piece - (piece > REACH_DEV), a, part, :] = value.astype(bf16)
        ret_one(p)
        gwp[cols, :] = lax.dot_general(
            att_v[:, cols], g_v[...], first_dim, preferred_element_type=f32
        ).astype(bf16)
        gw_one(p)

    def among(q, body):
        pl.when((q >= 0) & (q < pairs))(lambda: body(q))

    def step(p):
        pl.when((p >= 0) & (p + AHEAD_KV < pairs))(lambda: kv_start(p + AHEAD_KV))
        among(p + 2, kv_first)
        among(p + 1, kv_second)
        for lead in range(LEAD, 0, -1):
            among(p + lead, lambda q, lead=lead: w_hop(q, lead))
        pl.when(p == -2)(setup)

        @pl.when((p >= 0) & (p < pairs))
        def _():
            kv_wait(p)
            w_wait(p)
            attend(p)

        among(p - 1, ret_two)
        among(p - 1, gw_two)
        among(p - 2, ret_three)

        @pl.when(p == pairs)
        def _():
            mix_v[...] = jnp.dot(att_v[...], wbuf[...], preferred_element_type=f32).astype(bf16)
            pltpu.make_async_copy(mix_v, mixed_hbm, fin_sem.at[0]).start()

        among(p - 3, ret_four)
        for lag in range(2, LEAD + 1):
            among(p - lag, lambda q, lag=lag: gw_hop(q, lag))

    over(-LEAD, pairs + LEAD, step)

    gw_y().wait_recv()
    gwout[...] = (gfin[...] + ybuf[...].astype(f32)) * jnp.float32(1.0 / math.sqrt(tokens))
    pltpu.make_async_copy(gwout, gw_hbm, fin_sem.at[1]).start()

    w_y().wait_send()

    def sent(p):
        for a in range(2):
            kv_y(a, p).wait_send()
            kv_c(a, p).wait_send()
        pl.when(has_ahead)(lambda: kv_z(p).wait_send())
        pl.when(on_sent)(lambda: kv_on(p).wait_send())
        pl.when(sent_back)(lambda: back(p).wait_send())
        across(p).wait_send()
        pl.when(has_behind)(lambda: ret_z(p).wait_send())
        ret_y(p).wait_send()
        for a in range(3):
            out_copy(a, p).wait()
        for i in range(chips):
            chip = p * chips + i
            up, down = w_goes(chip)
            pl.when(up)(lambda chip=chip: w_z(chip, 1).wait_send())
            pl.when(down)(lambda chip=chip: w_z(chip, 0).wait_send())
            w_c(chip).wait_send()
            gw_c(chip).wait_send()
            pl.when(chip // 2 != z)(lambda chip=chip: gw_z(chip).wait_send())

    over(0, pairs, sent)
    gw_y().wait_send()
    pltpu.make_async_copy(mix_v, mixed_hbm, fin_sem.at[0]).wait()
    pltpu.make_async_copy(gwout, gw_hbm, fin_sem.at[1]).wait()


def layer(contacts, count, ids, queries, keys, values, weight, grad_output):
    n = lax.axis_size("ctx")
    rows, width = queries.shape
    blocks, listed = contacts.shape
    block = rows // blocks
    wrows = weight.shape[0]
    pairs = width // LANES
    window = (2 * REACH_DEV + 1) * blocks
    f32, bf16 = jnp.float32, jnp.bfloat16
    vmem, dma = pltpu.VMEM, pltpu.SemaphoreType.DMA
    smem = pl.BlockSpec(memory_space=pltpu.SMEM)
    hbm = pl.BlockSpec(memory_space=pl.ANY)
    slots = blocks * listed + 1
    flat, both = (rows, width), (pairs, 2, rows, LANES)
    return pl.pallas_call(
        functools.partial(layer_kernel, n, blocks, listed, block, width // HEADS, rows * n),
        in_specs=[smem, smem, pl.BlockSpec(memory_space=pltpu.VMEM)] + [hbm] * 5,
        out_specs=[hbm] * 5,
        out_shape=[jax.ShapeDtypeStruct(flat, bf16)] * 4 + [jax.ShapeDtypeStruct((wrows, width), f32)],
        scratch_shapes=[vmem(flat, bf16)] * 4
        + [
            vmem((width, width), bf16),
            vmem((pairs, 2 * REACH_DEV, 2, rows, LANES), bf16),
            vmem((window, block, block), f32),
            vmem((blocks * listed * block, LANES), f32),
            vmem((window, block, LANES), bf16),
            vmem((window, block, LANES), bf16),
            vmem((listed * block, LANES), bf16),
            vmem((listed * block, LANES), bf16),
            vmem((slots, block, LANES), f32),
            vmem((slots, block, LANES), f32),
            vmem(both, f32),
            vmem((pairs, 2 * REACH_DEV, 2, rows, LANES), bf16),
        ]
        + [vmem(both, bf16)] * 7
        + [
            vmem((pairs, rows, LANES), bf16),
            vmem(flat, bf16),
            vmem(flat, bf16),
            vmem((width, width), bf16),
            vmem((n // 2, wrows, width), bf16),
            vmem((n // 2, wrows, width), bf16),
            vmem((2, n // 2, wrows, width), bf16),
            vmem((wrows, width), bf16),
            vmem((wrows, width), bf16),
            vmem((wrows, width), f32),
            vmem((wrows, width), f32),
            pltpu.SMEM((blocks, 2 * REACH_DEV * blocks + 1), jnp.int32),
            dma((5,)),
        ]
        + [dma((2, pairs))] * 4
        + [dma((pairs,))] * 4
        + [dma, dma((2, n // 2))]
        + [dma((n // 2,))] * 3
        + [dma((4, pairs))] * 2
        + [dma((n // 2,))] * 3
        + [dma((2, n // 2)), dma, dma, dma((3, pairs)), dma((2,))],
        compiler_params=pltpu.CompilerParams(
            collective_id=0, has_side_effects=True, vmem_limit_bytes=60 * 1024 * 1024
        ),
        name="contact_layer",
    )(contacts, count, ids, queries, keys, values, weight, grad_output)


def shards(queries, keys, values, out_weight, grad_output, complex_id, contacts, contact_count):
    block = queries.shape[0] // contacts.shape[0]
    return layer(
        contacts, contact_count, complex_id.reshape(-1, block), queries, keys, values, out_weight, grad_output
    )


def solution(mesh):
    split = P(("groups", "ctx"), None)
    return jax.shard_map(
        shards,
        mesh=mesh,
        in_specs=(split, split, split, P("ctx", None), split, P("groups"), split, P(("groups", "ctx"))),
        out_specs=(split,) * 5,
        check_vma=False,
    )
```

```python
import functools
import math

import jax
import jax.numpy as jnp
from jax import lax
from jax.experimental import pallas as pl
from jax.experimental.pallas import tpu as pltpu
from jax.sharding import PartitionSpec as P

HEADS = 16
REACH_DEV = 2
LANES = 128
AHEAD_KV = 5


def layer_kernel(
    n, blocks, listed, block, head_dim, tokens,
    contacts, count, ids, q_hbm, k_hbm, v_hbm, w_hbm, g_hbm,
    mixed_hbm, dq_hbm, dk_hbm, dv_hbm, gw_hbm,
    q_v, k_v, v_v, g_v, wbuf, land, idt, bias, kwin, vwin, kg, vg, dks, dvs,
    own, far, got_f, got_c, got_z, got_y, put_z, put_y, outg, dqb, att_v, mix_v,
    gwp, core_got, gsum, gin, ysend, ybuf, gfin, gwout, inv,
    local_sem, y_s, y_r, c_s, c_r, z_s, z_r, o_s, o_r,
    wy_s, w_s, w_r, wc_s, wc_r, ret_s, ret_r, gc_s, gc_r, gz_s, gz_r, gy_s, gy_r,
    out_sem, fin_sem,
):
    f32, bf16 = jnp.float32, jnp.bfloat16
    rows = blocks * block
    width = q_hbm.shape[1]
    pairs = width // LANES
    wrows = w_hbm.shape[0]
    nz = n // 4
    chips = LANES // (2 * wrows)
    reach = REACH_DEV * blocks
    windows = (2 * REACH_DEV + 1) * blocks
    scale = 1.0 / math.sqrt(head_dim)

    me = lax.axis_index("ctx")
    core, y, z = lax.rem(me, 2), lax.rem(me // 2, 2), me // 4
    ypeer, cpeer = me + 2 - 4 * y, me + 1 - 2 * core
    ahead, behind = me + 4 - 8 * y, me - 4 + 8 * y
    has_ahead = (ahead >= 0) & (ahead < n)
    has_behind = (behind >= 0) & (behind < n)

    def remote(src, dst, send, recv, device):
        return pltpu.make_async_remote_copy(
            src_ref=src, dst_ref=dst, send_sem=send, recv_sem=recv,
            device_id={"ctx": device}, device_id_type=pl.DeviceIdType.MESH,
        )

    def over(start, stop, body):
        lax.fori_loop(start, stop, lambda i, c: (body(i), c)[1], 0)

    def turn(p):
        return p + 2 - 4 * lax.rem(p // 2, 2)

    def lanes(p):
        return pl.ds(pl.multiple_of(turn(p) * LANES, LANES), LANES)

    def shard(d):
        return pl.ds(pl.multiple_of(d * wrows, wrows), wrows)

    def kv_y(a, p):
        return remote(
            (k_hbm, v_hbm)[a].at[:, lanes(p)], land.at[p, 3 * y, a], y_s.at[a, p], y_r.at[a, p], ypeer
        )

    def kv_c(a, p):
        return remote(
            (k_hbm, v_hbm)[a].at[:, lanes(p)], land.at[p, 1 + core, a], c_s.at[a, p], c_r.at[a, p], cpeer
        )

    def kv_z(p):
        return remote(land.at[p, 3 - 3 * y], land.at[p, 3 * y], z_s.at[p], z_r.at[p], ahead)

    def kv_on(p):
        return remote(land.at[p, 3 - 3 * core], land.at[p, 2 - core], o_s.at[p], o_r.at[p], cpeer)

    on_sent = (y == core) | has_behind
    on_got = (y != core) | has_behind

    def kv_start(p):
        for a in range(2):
            kv_y(a, p).start()
        for a in range(2):
            kv_c(a, p).start()

    def kv_first(p):
        for a in range(2):
            kv_y(a, p).wait_recv()
        pl.when(has_ahead)(lambda: kv_z(p).start())
        pl.when(y == core)(lambda: kv_on(p).start())

    def kv_second(p):
        @pl.when(has_behind)
        def _():
            kv_z(p).wait_recv()
            pl.when(y != core)(lambda: kv_on(p).start())

    def kv_wait(p):
        for a in range(2):
            kv_c(a, p).wait_recv()
        pl.when(on_got)(lambda: kv_on(p).wait_recv())

    mychip = me // 2

    def w_y():
        return remote(w_hbm, wbuf.at[shard(me)], wy_s, w_r.at[mychip], ypeer)

    def w_in(chip):
        d = shard(2 * chip + core)
        return remote(wbuf.at[d], wbuf.at[d], wy_s, w_r.at[chip], ypeer)

    def w_z(chip, up):
        d = shard(2 * chip + core)
        return remote(wbuf.at[d], wbuf.at[d], w_s.at[up, chip], w_r.at[chip], me - 4 + 8 * up)

    def w_c(chip):
        d = shard(2 * chip + core)
        return remote(wbuf.at[d], wbuf.at[d], wc_s.at[chip], wc_r.at[chip], cpeer)

    def w_goes(chip):
        zc = chip // 2
        return (z >= zc) & (z + 1 < nz), (z <= zc) & (z > 0)

    def w_hops(now):
        def visit(q):
            for i in range(chips):
                chip = turn(q) * chips + i
                far_off = jnp.minimum(jnp.abs(z - chip // 2), 3)
                late = jnp.where(q < 2, far_off - 3, jnp.where(q < 4, far_off - 2, 2 * far_off - 3))
                late = jnp.where(q < 6, late, 2 * far_off - 1)

                @pl.when(jnp.where(far_off == 0, -3, late) == now)
                def _(chip=chip):
                    up, down = w_goes(chip)
                    pl.when(chip != mychip)(lambda: w_in(chip).wait_recv())
                    pl.when(up)(lambda: w_z(chip, 1).start())
                    pl.when(down)(lambda: w_z(chip, 0).start())
                    w_c(chip).start()

        over(0, pairs, visit)

    def w_wait(p):
        for i in range(chips):
            w_c(turn(p) * chips + i).wait_recv()

    def back(p):
        return remote(far.at[p, 1 + core], got_f.at[p], ret_s.at[0, p], ret_r.at[0, p], cpeer)

    def across(p):
        return remote(far.at[p, 2 - core], got_c.at[p], ret_s.at[1, p], ret_r.at[1, p], cpeer)

    def ret_z(p):
        return remote(put_z.at[p], got_z.at[p], ret_s.at[2, p], ret_r.at[2, p], behind)

    def ret_y(p):
        return remote(put_y.at[p], got_y.at[p], ret_s.at[3, p], ret_r.at[3, p], ypeer)

    sent_back = (y != core) | has_behind
    got_back = (y == core) | has_behind

    def ret_one(p):
        pl.when(sent_back)(lambda: back(p).start())
        across(p).start()

    def ret_two(p):
        pl.when(got_back)(lambda: back(p).wait_recv())
        value = far[p, 3 * y].astype(f32)
        put_z[p] = (value + jnp.where(y != core, got_f[p].astype(f32), 0.0)).astype(bf16)
        pl.when(has_behind)(lambda: ret_z(p).start())

    def ret_three(p):
        pl.when(has_ahead)(lambda: ret_z(p).wait_recv())
        value = far[p, 3 - 3 * y].astype(f32)
        value = value + jnp.where(has_ahead, got_z[p].astype(f32), 0.0)
        value = value + jnp.where(y == core, got_f[p].astype(f32), 0.0)
        put_y[p] = value.astype(bf16)
        ret_y(p).start()

    def out_copy(a, p):
        src = dqb.at[p] if a == 2 else outg.at[p, a]
        return pltpu.make_async_copy(src, (dk_hbm, dv_hbm, dq_hbm)[a].at[:, lanes(p)], out_sem.at[a, p])

    def ret_four(p):
        across(p).wait_recv()
        ret_y(p).wait_recv()
        outg[p] = (own[p] + got_c[p].astype(f32) + got_y[p].astype(f32)).astype(bf16)
        for a in range(2):
            out_copy(a, p).start()

    def gw_c(chip):
        return remote(
            gwp.at[shard(2 * chip + 1 - core)], core_got.at[chip], gc_s.at[chip], gc_r.at[chip], cpeer
        )

    def gw_z(chip):
        side = (z > chip // 2).astype(jnp.int32)
        return remote(
            gsum.at[chip], gin.at[side, chip], gz_s.at[chip], gz_r.at[side, chip], me + 4 - 8 * side
        )

    def gw_in(chip, side):
        return remote(gsum.at[chip], gin.at[side, chip], gz_s.at[chip], gz_r.at[side, chip], ypeer)

    def gw_y():
        return remote(ysend, ybuf, gy_s, gy_r, ypeer)

    def gw_one(p):
        for i in range(chips):
            gw_c(turn(p) * chips + i).start()

    def gw_two(p):
        for i in range(chips):
            chip = turn(p) * chips + i
            zc = chip // 2
            gw_c(chip).wait_recv()
            value = gwp[shard(2 * chip + core), :].astype(f32) + core_got[chip].astype(f32)
            gsum[chip] = value.astype(bf16)
            ends = ((z == 0) & (zc > 0)) | ((z == nz - 1) & (zc < nz - 1))
            pl.when(ends)(lambda chip=chip: gw_z(chip).start())

    def gw_hop(p, lag):
        for i in range(chips):
            chip = turn(p) * chips + i
            zc = chip // 2
            stage = jnp.where(z < zc, z, nz - 1 - z)

            @pl.when((z != zc) & (stage > 0) & (2 * jnp.minimum(stage, 2) + 1 == lag))
            def _(chip=chip, zc=zc):
                side = (z > zc).astype(jnp.int32)
                gw_in(chip, side).wait_recv()
                gsum[chip] = (gsum[chip].astype(f32) + gin[side, chip].astype(f32)).astype(bf16)
                gw_z(chip).start()

            @pl.when((z == zc) & (2 * jnp.minimum(jnp.maximum(zc, nz - 1 - zc), 3) + 1 == lag))
            def _(chip=chip):
                yc = lax.rem(chip, 2)
                pl.when(z > 0)(lambda: gw_in(chip, 0).wait_recv())
                pl.when(z < nz - 1)(lambda: gw_in(chip, 1).wait_recv())
                value = gsum[chip].astype(f32)
                value = value + jnp.where(z > 0, gin[0, chip].astype(f32), 0.0)
                value = value + jnp.where(z < nz - 1, gin[1, chip].astype(f32), 0.0)

                @pl.when(yc == y)
                def _():
                    gfin[...] = value

                @pl.when(yc != y)
                def _():
                    ysend[...] = value.astype(bf16)
                    gw_y().start()

    barrier = pltpu.get_barrier_semaphore()

    def hello(device):
        pl.semaphore_signal(barrier, inc=1, device_id={"ctx": device}, device_id_type=pl.DeviceIdType.MESH)

    hello(ypeer)
    hello(cpeer)
    pl.when(z > 0)(lambda: hello(me - 4))
    pl.when(z < nz - 1)(lambda: hello(me + 4))
    pl.semaphore_wait(barrier, 2 + (z > 0).astype(jnp.int32) + (z < nz - 1).astype(jnp.int32))

    def urgent(p):
        return mychip // chips == turn(p)

    loads = [
        pltpu.make_async_copy(w_hbm, wbuf.at[shard(me)], local_sem.at[0]),
        pltpu.make_async_copy(g_hbm, g_v, local_sem.at[1]),
        pltpu.make_async_copy(q_hbm, q_v, local_sem.at[2]),
        pltpu.make_async_copy(k_hbm, k_v, local_sem.at[3]),
        pltpu.make_async_copy(v_hbm, v_v, local_sem.at[4]),
    ]
    loads[0].start()
    pl.when(urgent(0))(lambda: w_y().start())
    kv_start(0)
    pl.when(jnp.logical_not(urgent(0)))(lambda: w_y().start())
    for copy in loads[1:]:
        copy.start()
    loads[0].wait()

    first = me * blocks - reach

    def setup():
        total_blocks = ids.shape[0]
        for w in range(windows):
            at = jnp.clip(first + w, 0, total_blocks - 1)
            row = ids[pl.ds(at, 1), :].astype(f32)
            idt[w] = jnp.broadcast_to(row, (block, block)).T
        local = [[jnp.clip(contacts[b, j] - first, 0, windows - 1) for j in range(listed)] for b in range(blocks)]
        for b in range(blocks):
            mine = ids[pl.ds(me * blocks + b, 1), :].astype(f32)
            for j in range(listed):
                same = idt[local[b][j]] == mine
                alive = jnp.full((block, LANES), count[b], jnp.int32) > j
                bias[pl.ds((b * listed + j) * block, block), :] = jnp.where(same & alive, 0.0, -jnp.inf)
            for w in range(2 * reach + 1):
                slot = jnp.int32(blocks * listed)
                for j in range(listed):
                    slot = jnp.where(local[b][j] == w + b, b * listed + j, slot)
                inv[b, w] = slot
        for ref in (dks, dvs):
            ref[blocks * listed] = jnp.zeros((block, LANES), f32)
        for copy in loads[1:]:
            copy.wait()

    lane = lax.broadcasted_iota(jnp.int32, (block, LANES), 1) < head_dim
    sub = lax.broadcasted_iota(jnp.int32, (LANES, block), 0) < head_dim
    last_dim = (((1,), (1,)), ((), ()))
    first_dim = (((0,), (0,)), ((), ()))

    def two(x):
        zero = jnp.zeros_like(x)
        return jnp.concatenate([jnp.where(lane, x, zero), jnp.where(lane, zero, x)], axis=0).astype(bf16)

    def among(q, body):
        pl.when((q >= 0) & (q < pairs))(lambda: body(q))

    def gw_hops(p):
        for lag in (3, 5, 7):
            among(p - lag, lambda q, lag=lag: gw_hop(q, lag))

    def serve(p):
        among(p + AHEAD_KV, kv_start)
        among(p - 1, ret_two)
        among(p + 3, kv_first)
        among(p - 3, ret_three)
        among(p + 1, kv_second)
        w_hops(p)
        among(p - 1, gw_two)
        gw_hops(p)
        among(p - 6, ret_four)

    def attend(p):
        cols = lanes(p)
        grad_all = lax.dot_general(
            g_v[...], wbuf[cols, :], last_dim, preferred_element_type=f32
        ).astype(bf16)
        for i, piece in enumerate((0, 1, None, 2, 3)):
            span = pl.ds(i * blocks, blocks)
            kwin[span] = (k_v[:, cols] if piece is None else land[p, piece, 0]).reshape(blocks, block, LANES)
            vwin[span] = (v_v[:, cols] if piece is None else land[p, piece, 1]).reshape(blocks, block, LANES)
        for b in range(blocks):
            if b == blocks - 1:
                serve(p)
            here = pl.ds(b * block, block)
            for j in range(listed):
                at = jnp.clip(contacts[b, j] - first, 0, windows - 1)
                kg[pl.ds(j * block, block), :] = kwin[at]
                vg[pl.ds(j * block, block), :] = vwin[at]
            grad = grad_all[b * block : (b + 1) * block].astype(f32)
            q2 = two(q_v[here, cols].astype(f32) * scale)
            d2 = two(grad)
            s = lax.dot_general(kg[...], q2, last_dim, preferred_element_type=f32)
            mask = bias[pl.ds(b * listed * block, listed * block), :]
            s = s + jnp.concatenate([mask, mask], axis=1)
            top = jnp.max(s, axis=0, keepdims=True)
            e = jnp.exp(s - top)
            probs = e * (1.0 / jnp.sum(e, axis=0, keepdims=True))
            low = probs.astype(bf16)
            ot = lax.dot_general(vg[...], low, first_dim, preferred_element_type=f32)
            att = jnp.where(sub, ot[:, :block], ot[:, block:]).astype(bf16).astype(f32)
            att_v[here, cols] = att.T.astype(bf16)
            prod = grad.T * att
            row_dot = jnp.concatenate(
                [jnp.sum(prod[:head_dim], axis=0, keepdims=True), jnp.sum(prod[head_dim:], axis=0, keepdims=True)],
                axis=1,
            )
            dp = lax.dot_general(vg[...], d2, last_dim, preferred_element_type=f32)
            ds = (probs * (dp - row_dot)).astype(bf16)
            dqt = lax.dot_general(kg[...], ds, first_dim, preferred_element_type=f32)
            dq = jnp.where(sub, dqt[:, :block], dqt[:, block:]) * scale
            dqb[p, here, :] = dq.T.astype(bf16)
            part = pl.ds(b * listed, listed)
            dks[part] = jnp.dot(ds, q2, preferred_element_type=f32).reshape(listed, block, LANES)
            dvs[part] = jnp.dot(low, d2, preferred_element_type=f32).reshape(listed, block, LANES)
        out_copy(2, p).start()
        for a, slots in enumerate((dks, dvs)):
            for w in range(windows):
                value = None
                for b in range(blocks):
                    if 0 <= w - b <= 2 * reach:
                        term = slots[inv[b, w - b]]
                        value = term if value is None else value + term
                piece, part = w // blocks, pl.ds((w % blocks) * block, block)
                if piece == REACH_DEV:
                    own[p, a, part, :] = value
                else:
                    far[p, piece - (piece > REACH_DEV), a, part, :] = value.astype(bf16)
        ret_one(p)
        gwp[cols, :] = lax.dot_general(
            att_v[:, cols], g_v[...], first_dim, preferred_element_type=f32
        ).astype(bf16)
        gw_one(p)

    def step(p):
        kv_wait(p)
        w_wait(p)
        attend(p)

    w_hops(jnp.int32(-3))
    for p in range(1, AHEAD_KV):
        kv_start(p)
    setup()
    w_hops(jnp.int32(-2))
    kv_first(0)
    w_hops(jnp.int32(-1))
    kv_first(1)
    kv_second(0)
    kv_first(2)
    over(0, pairs, step)
    done = jnp.int32(pairs)
    ret_two(done - 1)
    ret_three(done - 3)
    gw_two(done - 1)
    gw_hops(done)
    ret_three(done - 2)
    mix_v[...] = jnp.dot(att_v[...], wbuf[...], preferred_element_type=f32).astype(bf16)
    pltpu.make_async_copy(mix_v, mixed_hbm, fin_sem.at[0]).start()
    gw_hops(done + 1)
    ret_three(done - 1)
    gw_hops(done + 2)
    ret_four(done - 6)
    ret_four(done - 5)
    gw_hops(done + 3)
    ret_four(done - 4)
    gw_hops(done + 4)
    gw_hops(done + 5)
    gw_hops(done + 6)
    ret_four(done - 3)
    ret_four(done - 2)
    ret_four(done - 1)

    gw_y().wait_recv()
    gwout[...] = (gfin[...] + ybuf[...].astype(f32)) * jnp.float32(1.0 / math.sqrt(tokens))
    pltpu.make_async_copy(gwout, gw_hbm, fin_sem.at[1]).start()

    w_y().wait_send()

    def sent(p):
        for a in range(2):
            kv_y(a, p).wait_send()
            kv_c(a, p).wait_send()
        pl.when(has_ahead)(lambda: kv_z(p).wait_send())
        pl.when(on_sent)(lambda: kv_on(p).wait_send())
        pl.when(sent_back)(lambda: back(p).wait_send())
        across(p).wait_send()
        pl.when(has_behind)(lambda: ret_z(p).wait_send())
        ret_y(p).wait_send()
        for a in range(3):
            out_copy(a, p).wait()
        for i in range(chips):
            chip = p * chips + i
            up, down = w_goes(chip)
            pl.when(up)(lambda chip=chip: w_z(chip, 1).wait_send())
            pl.when(down)(lambda chip=chip: w_z(chip, 0).wait_send())
            w_c(chip).wait_send()
            gw_c(chip).wait_send()
            pl.when(chip // 2 != z)(lambda chip=chip: gw_z(chip).wait_send())

    over(0, pairs, sent)
    gw_y().wait_send()
    pltpu.make_async_copy(mix_v, mixed_hbm, fin_sem.at[0]).wait()
    pltpu.make_async_copy(gwout, gw_hbm, fin_sem.at[1]).wait()


def layer(contacts, count, ids, queries, keys, values, weight, grad_output):
    n = lax.axis_size("ctx")
    rows, width = queries.shape
    blocks, listed = contacts.shape
    block = rows // blocks
    wrows = weight.shape[0]
    pairs = width // LANES
    window = (2 * REACH_DEV + 1) * blocks
    f32, bf16 = jnp.float32, jnp.bfloat16
    vmem, dma = pltpu.VMEM, pltpu.SemaphoreType.DMA
    smem = pl.BlockSpec(memory_space=pltpu.SMEM)
    hbm = pl.BlockSpec(memory_space=pl.ANY)
    slots = blocks * listed + 1
    flat, both = (rows, width), (pairs, 2, rows, LANES)
    return pl.pallas_call(
        functools.partial(layer_kernel, n, blocks, listed, block, width // HEADS, rows * n),
        in_specs=[smem, smem, pl.BlockSpec(memory_space=pltpu.VMEM)] + [hbm] * 5,
        out_specs=[hbm] * 5,
        out_shape=[jax.ShapeDtypeStruct(flat, bf16)] * 4 + [jax.ShapeDtypeStruct((wrows, width), f32)],
        scratch_shapes=[vmem(flat, bf16)] * 4
        + [
            vmem((width, width), bf16),
            vmem((pairs, 2 * REACH_DEV, 2, rows, LANES), bf16),
            vmem((window, block, block), f32),
            vmem((blocks * listed * block, LANES), f32),
            vmem((window, block, LANES), bf16),
            vmem((window, block, LANES), bf16),
            vmem((listed * block, LANES), bf16),
            vmem((listed * block, LANES), bf16),
            vmem((slots, block, LANES), f32),
            vmem((slots, block, LANES), f32),
            vmem(both, f32),
            vmem((pairs, 2 * REACH_DEV, 2, rows, LANES), bf16),
        ]
        + [vmem(both, bf16)] * 7
        + [
            vmem((pairs, rows, LANES), bf16),
            vmem(flat, bf16),
            vmem(flat, bf16),
            vmem((width, width), bf16),
            vmem((n // 2, wrows, width), bf16),
            vmem((n // 2, wrows, width), bf16),
            vmem((2, n // 2, wrows, width), bf16),
            vmem((wrows, width), bf16),
            vmem((wrows, width), bf16),
            vmem((wrows, width), f32),
            vmem((wrows, width), f32),
            pltpu.SMEM((blocks, 2 * REACH_DEV * blocks + 1), jnp.int32),
            dma((5,)),
        ]
        + [dma((2, pairs))] * 4
        + [dma((pairs,))] * 4
        + [dma, dma((2, n // 2))]
        + [dma((n // 2,))] * 3
        + [dma((4, pairs))] * 2
        + [dma((n // 2,))] * 3
        + [dma((2, n // 2)), dma, dma, dma((3, pairs)), dma((2,))],
        compiler_params=pltpu.CompilerParams(
            collective_id=0, has_side_effects=True, vmem_limit_bytes=60 * 1024 * 1024
        ),
        name="contact_layer",
    )(contacts, count, ids, queries, keys, values, weight, grad_output)


def hand_over_kernel(*refs):
    for src, dst in zip(refs[: len(refs) // 2], refs[len(refs) // 2 :]):
        dst[...] = src[...]


def hand_over(arrays, parts=2):
    specs = [pl.BlockSpec((a.shape[0] // parts, a.shape[1]), lambda i: (i, 0)) for a in arrays]
    return pl.pallas_call(
        hand_over_kernel,
        grid=(parts,),
        in_specs=specs,
        out_specs=specs,
        out_shape=[jax.ShapeDtypeStruct(a.shape, a.dtype) for a in arrays],
        name="hand_over",
    )(*arrays)


def shards(queries, keys, values, out_weight, grad_output, complex_id, contacts, contact_count):
    block = queries.shape[0] // contacts.shape[0]
    return hand_over(
        layer(contacts, contact_count, complex_id.reshape(-1, block), queries, keys, values, out_weight, grad_output)
    )


def solution(mesh):
    split = P(("groups", "ctx"), None)
    return jax.shard_map(
        shards,
        mesh=mesh,
        in_specs=(split, split, split, P("ctx", None), split, P("groups"), split, P(("groups", "ctx"))),
        out_specs=(split,) * 5,
        check_vma=False,
    )
```

```python
import functools
import math

import jax
import jax.numpy as jnp
from jax import lax
from jax.experimental import pallas as pl
from jax.experimental.pallas import tpu as pltpu
from jax.sharding import PartitionSpec as P

HEADS = 16
REACH_DEV = 2
LANES = 128
AHEAD_KV = 5


def layer_kernel(
    n, blocks, listed, block, head_dim, tokens,
    contacts, count, ids, q_hbm, k_hbm, v_hbm, w_hbm, g_hbm,
    mixed_hbm, dq_hbm, dk_hbm, dv_hbm, gw_hbm,
    q_v, k_v, v_v, g_v, wbuf, land, idt, bias, kwin, vwin, kg, vg, dks, dvs,
    own, far, got_f, got_c, got_z, got_y, put_z, put_y, outg, dqb, att_v, mix_v,
    gwp, core_got, gsum, gin, ysend, ybuf, gfin, gwout, inv,
    local_sem, y_s, y_r, c_s, c_r, z_s, z_r, o_s, o_r,
    wy_s, w_s, w_r, wc_s, wc_r, ret_s, ret_r, gc_s, gc_r, gz_s, gz_r, gy_s, gy_r,
    out_sem, fin_sem,
):
    f32, bf16 = jnp.float32, jnp.bfloat16
    rows = blocks * block
    width = q_hbm.shape[1]
    pairs = width // LANES
    wrows = w_hbm.shape[0]
    nz = n // 4
    chips = LANES // (2 * wrows)
    reach = REACH_DEV * blocks
    windows = (2 * REACH_DEV + 1) * blocks
    scale = 1.0 / math.sqrt(head_dim)

    me = lax.axis_index("ctx")
    core, y, z = lax.rem(me, 2), lax.rem(me // 2, 2), me // 4
    ypeer, cpeer = me + 2 - 4 * y, me + 1 - 2 * core
    ahead, behind = me + 4 - 8 * y, me - 4 + 8 * y
    has_ahead = (ahead >= 0) & (ahead < n)
    has_behind = (behind >= 0) & (behind < n)

    def remote(src, dst, send, recv, device):
        return pltpu.make_async_remote_copy(
            src_ref=src, dst_ref=dst, send_sem=send, recv_sem=recv,
            device_id={"ctx": device}, device_id_type=pl.DeviceIdType.MESH,
        )

    def over(start, stop, body):
        lax.fori_loop(start, stop, lambda i, c: (body(i), c)[1], 0)

    def turn(p):
        return p + 2 - 4 * lax.rem(p // 2, 2)

    def lanes(p):
        return pl.ds(pl.multiple_of(turn(p) * LANES, LANES), LANES)

    def shard(d):
        return pl.ds(pl.multiple_of(d * wrows, wrows), wrows)

    def kv_y(a, p):
        return remote(
            (k_hbm, v_hbm)[a].at[:, lanes(p)], land.at[p, 3 * y, a], y_s.at[a, p], y_r.at[a, p], ypeer
        )

    def kv_c(a, p):
        return remote(
            (k_hbm, v_hbm)[a].at[:, lanes(p)], land.at[p, 1 + core, a], c_s.at[a, p], c_r.at[a, p], cpeer
        )

    def kv_z(p):
        return remote(land.at[p, 3 - 3 * y], land.at[p, 3 * y], z_s.at[p], z_r.at[p], ahead)

    def kv_on(p):
        return remote(land.at[p, 3 - 3 * core], land.at[p, 2 - core], o_s.at[p], o_r.at[p], cpeer)

    on_sent = (y == core) | has_behind
    on_got = (y != core) | has_behind

    def kv_start(p):
        for a in range(2):
            kv_y(a, p).start()
        for a in range(2):
            kv_c(a, p).start()

    def kv_first(p):
        for a in range(2):
            kv_y(a, p).wait_recv()
        pl.when(has_ahead)(lambda: kv_z(p).start())
        pl.when(y == core)(lambda: kv_on(p).start())

    def kv_second(p):
        @pl.when(has_behind)
        def _():
            kv_z(p).wait_recv()
            pl.when(y != core)(lambda: kv_on(p).start())

    def kv_wait(p):
        for a in range(2):
            kv_c(a, p).wait_recv()
        pl.when(on_got)(lambda: kv_on(p).wait_recv())

    mychip = me // 2

    def w_y():
        return remote(w_hbm, wbuf.at[shard(me)], wy_s, w_r.at[mychip], ypeer)

    def w_in(chip):
        d = shard(2 * chip + core)
        return remote(wbuf.at[d], wbuf.at[d], wy_s, w_r.at[chip], ypeer)

    def w_z(chip, up):
        d = shard(2 * chip + core)
        return remote(wbuf.at[d], wbuf.at[d], w_s.at[up, chip], w_r.at[chip], me - 4 + 8 * up)

    def w_c(chip):
        d = shard(2 * chip + core)
        return remote(wbuf.at[d], wbuf.at[d], wc_s.at[chip], wc_r.at[chip], cpeer)

    def w_goes(chip):
        zc = chip // 2
        return (z >= zc) & (z + 1 < nz), (z <= zc) & (z > 0)

    def w_hops(now, start=0):
        def visit(q):
            for i in range(chips):
                chip = turn(q) * chips + i
                far_off = jnp.minimum(jnp.abs(z - chip // 2), 3)
                late = jnp.where(q < 1, jnp.minimum(far_off, 2) - 3, jnp.where(q < 4, far_off - 2, 2 * far_off - 3))
                late = jnp.where(q < 6, late, 2 * far_off - 1)
                near = jnp.where(q < 1, -3, jnp.where(q < 4, -2, -1))
                near = jnp.where(chip == mychip, -4, near)

                @pl.when(jnp.where(far_off == 0, near, late) == now)
                def _(chip=chip):
                    up, down = w_goes(chip)
                    pl.when(chip != mychip)(lambda: w_in(chip).wait_recv())
                    pl.when(up)(lambda: w_z(chip, 1).start())
                    pl.when(down)(lambda: w_z(chip, 0).start())
                    w_c(chip).start()

        over(start, pairs, visit)

    def w_wait(p):
        for i in range(chips):
            w_c(turn(p) * chips + i).wait_recv()

    def back(p):
        return remote(far.at[p, 1 + core], got_f.at[p], ret_s.at[0, p], ret_r.at[0, p], cpeer)

    def across(p):
        return remote(far.at[p, 2 - core], got_c.at[p], ret_s.at[1, p], ret_r.at[1, p], cpeer)

    def ret_z(p):
        return remote(put_z.at[p], got_z.at[p], ret_s.at[2, p], ret_r.at[2, p], behind)

    def ret_y(p):
        return remote(put_y.at[p], got_y.at[p], ret_s.at[3, p], ret_r.at[3, p], ypeer)

    sent_back = (y != core) | has_behind
    got_back = (y == core) | has_behind

    def ret_one(p):
        pl.when(sent_back)(lambda: back(p).start())
        across(p).start()

    def ret_two(p):
        pl.when(got_back)(lambda: back(p).wait_recv())
        value = far[p, 3 * y].astype(f32)
        put_z[p] = (value + jnp.where(y != core, got_f[p].astype(f32), 0.0)).astype(bf16)
        pl.when(has_behind)(lambda: ret_z(p).start())

    def ret_three(p):
        pl.when(has_ahead)(lambda: ret_z(p).wait_recv())
        value = far[p, 3 - 3 * y].astype(f32)
        value = value + jnp.where(has_ahead, got_z[p].astype(f32), 0.0)
        value = value + jnp.where(y == core, got_f[p].astype(f32), 0.0)
        put_y[p] = value.astype(bf16)
        ret_y(p).start()

    def out_copy(a, p):
        src = dqb.at[p] if a == 2 else outg.at[p, a]
        return pltpu.make_async_copy(src, (dk_hbm, dv_hbm, dq_hbm)[a].at[:, lanes(p)], out_sem.at[a, p])

    def ret_four(p):
        across(p).wait_recv()
        ret_y(p).wait_recv()
        outg[p] = (own[p] + got_c[p].astype(f32) + got_y[p].astype(f32)).astype(bf16)
        for a in range(2):
            out_copy(a, p).start()

    def gw_c(chip):
        return remote(
            gwp.at[shard(2 * chip + 1 - core)], core_got.at[chip], gc_s.at[chip], gc_r.at[chip], cpeer
        )

    def gw_z(chip):
        side = (z > chip // 2).astype(jnp.int32)
        return remote(
            gsum.at[chip], gin.at[side, chip], gz_s.at[chip], gz_r.at[side, chip], me + 4 - 8 * side
        )

    def gw_in(chip, side):
        return remote(gsum.at[chip], gin.at[side, chip], gz_s.at[chip], gz_r.at[side, chip], ypeer)

    def gw_y():
        return remote(ysend, ybuf, gy_s, gy_r, ypeer)

    def gw_one(p):
        for i in range(chips):
            gw_c(turn(p) * chips + i).start()

    def gw_two(p):
        for i in range(chips):
            chip = turn(p) * chips + i
            zc = chip // 2
            gw_c(chip).wait_recv()
            value = gwp[shard(2 * chip + core), :].astype(f32) + core_got[chip].astype(f32)
            gsum[chip] = value.astype(bf16)
            ends = ((z == 0) & (zc > 0)) | ((z == nz - 1) & (zc < nz - 1))
            pl.when(ends)(lambda chip=chip: gw_z(chip).start())

    def gw_hop(p, lag):
        for i in range(chips):
            chip = turn(p) * chips + i
            zc = chip // 2
            stage = jnp.where(z < zc, z, nz - 1 - z)

            @pl.when((z != zc) & (stage > 0) & (2 * jnp.minimum(stage, 2) + 1 == lag))
            def _(chip=chip, zc=zc):
                side = (z > zc).astype(jnp.int32)
                gw_in(chip, side).wait_recv()
                gsum[chip] = (gsum[chip].astype(f32) + gin[side, chip].astype(f32)).astype(bf16)
                gw_z(chip).start()

            @pl.when((z == zc) & (2 * jnp.minimum(jnp.maximum(zc, nz - 1 - zc), 3) + 1 == lag))
            def _(chip=chip):
                yc = lax.rem(chip, 2)
                pl.when(z > 0)(lambda: gw_in(chip, 0).wait_recv())
                pl.when(z < nz - 1)(lambda: gw_in(chip, 1).wait_recv())
                value = gsum[chip].astype(f32)
                value = value + jnp.where(z > 0, gin[0, chip].astype(f32), 0.0)
                value = value + jnp.where(z < nz - 1, gin[1, chip].astype(f32), 0.0)

                @pl.when(yc == y)
                def _():
                    gfin[...] = value

                @pl.when(yc != y)
                def _():
                    ysend[...] = value.astype(bf16)
                    gw_y().start()

    barrier = pltpu.get_barrier_semaphore()

    def hello(device):
        pl.semaphore_signal(barrier, inc=1, device_id={"ctx": device}, device_id_type=pl.DeviceIdType.MESH)

    hello(ypeer)
    hello(cpeer)
    pl.when(z > 0)(lambda: hello(me - 4))
    pl.when(z < nz - 1)(lambda: hello(me + 4))
    pl.semaphore_wait(barrier, 2 + (z > 0).astype(jnp.int32) + (z < nz - 1).astype(jnp.int32))

    def urgent(p):
        return mychip // chips == turn(p)

    loads = [
        pltpu.make_async_copy(w_hbm, wbuf.at[shard(me)], local_sem.at[0]),
        pltpu.make_async_copy(g_hbm, g_v, local_sem.at[1]),
        pltpu.make_async_copy(q_hbm, q_v, local_sem.at[2]),
        pltpu.make_async_copy(k_hbm, k_v, local_sem.at[3]),
        pltpu.make_async_copy(v_hbm, v_v, local_sem.at[4]),
    ]
    loads[0].start()
    pl.when(urgent(0))(lambda: w_y().start())
    kv_start(0)
    pl.when(jnp.logical_not(urgent(0)))(lambda: w_y().start())
    for copy in loads[1:]:
        copy.start()
    loads[0].wait()

    first = me * blocks - reach

    def setup():
        total_blocks = ids.shape[0]
        for w in range(windows):
            at = jnp.clip(first + w, 0, total_blocks - 1)
            row = ids[pl.ds(at, 1), :].astype(f32)
            idt[w] = jnp.broadcast_to(row, (block, block)).T
        local = [[jnp.clip(contacts[b, j] - first, 0, windows - 1) for j in range(listed)] for b in range(blocks)]
        for b in range(blocks):
            mine = ids[pl.ds(me * blocks + b, 1), :].astype(f32)
            for j in range(listed):
                same = idt[local[b][j]] == mine
                alive = jnp.full((block, LANES), count[b], jnp.int32) > j
                bias[pl.ds((b * listed + j) * block, block), :] = jnp.where(same & alive, 0.0, -jnp.inf)
            for w in range(2 * reach + 1):
                slot = jnp.int32(blocks * listed)
                for j in range(listed):
                    slot = jnp.where(local[b][j] == w + b, b * listed + j, slot)
                inv[b, w] = slot
        for ref in (dks, dvs):
            ref[blocks * listed] = jnp.zeros((block, LANES), f32)
        for copy in loads[1:]:
            copy.wait()

    lane = lax.broadcasted_iota(jnp.int32, (block, LANES), 1) < head_dim
    sub = lax.broadcasted_iota(jnp.int32, (LANES, block), 0) < head_dim
    last_dim = (((1,), (1,)), ((), ()))
    first_dim = (((0,), (0,)), ((), ()))

    def two(x):
        zero = jnp.zeros_like(x)
        return jnp.concatenate([jnp.where(lane, x, zero), jnp.where(lane, zero, x)], axis=0).astype(bf16)

    def among(q, body):
        pl.when((q >= 0) & (q < pairs))(lambda: body(q))

    def gw_hops(p):
        for lag in (3, 5, 7):
            among(p - lag, lambda q, lag=lag: gw_hop(q, lag))

    def serve(p):
        among(p + AHEAD_KV, kv_start)
        among(p - 1, ret_two)
        among(p + 3, kv_first)
        among(p - 3, ret_three)
        among(p + 1, kv_second)
        pl.when(p < 6)(lambda: w_hops(p, 1))
        among(p - 1, gw_two)
        gw_hops(p)
        among(p - 6, ret_four)

    def attend(p):
        cols = lanes(p)
        grad_all = lax.dot_general(
            g_v[...], wbuf[cols, :], last_dim, preferred_element_type=f32
        ).astype(bf16)
        for i, piece in enumerate((0, 1, None, 2, 3)):
            span = pl.ds(i * blocks, blocks)
            kwin[span] = (k_v[:, cols] if piece is None else land[p, piece, 0]).reshape(blocks, block, LANES)
            vwin[span] = (v_v[:, cols] if piece is None else land[p, piece, 1]).reshape(blocks, block, LANES)
        for b in range(blocks):
            if b == blocks - 1:
                serve(p)
            here = pl.ds(b * block, block)
            for j in range(listed):
                at = jnp.clip(contacts[b, j] - first, 0, windows - 1)
                kg[pl.ds(j * block, block), :] = kwin[at]
                vg[pl.ds(j * block, block), :] = vwin[at]
            grad = grad_all[b * block : (b + 1) * block].astype(f32)
            q2 = two(q_v[here, cols].astype(f32) * scale)
            d2 = two(grad)
            s = lax.dot_general(kg[...], q2, last_dim, preferred_element_type=f32)
            mask = bias[pl.ds(b * listed * block, listed * block), :]
            s = s + jnp.concatenate([mask, mask], axis=1)
            top = jnp.max(s, axis=0, keepdims=True)
            e = jnp.exp(s - top)
            probs = e * (1.0 / jnp.sum(e, axis=0, keepdims=True))
            low = probs.astype(bf16)
            ot = lax.dot_general(vg[...], low, first_dim, preferred_element_type=f32)
            att = jnp.where(sub, ot[:, :block], ot[:, block:]).astype(bf16).astype(f32)
            att_v[here, cols] = att.T.astype(bf16)
            prod = grad.T * att
            row_dot = jnp.concatenate(
                [jnp.sum(prod[:head_dim], axis=0, keepdims=True), jnp.sum(prod[head_dim:], axis=0, keepdims=True)],
                axis=1,
            )
            dp = lax.dot_general(vg[...], d2, last_dim, preferred_element_type=f32)
            ds = (probs * (dp - row_dot)).astype(bf16)
            dqt = lax.dot_general(kg[...], ds, first_dim, preferred_element_type=f32)
            dq = jnp.where(sub, dqt[:, :block], dqt[:, block:]) * scale
            dqb[p, here, :] = dq.T.astype(bf16)
            part = pl.ds(b * listed, listed)
            dks[part] = jnp.dot(ds, q2, preferred_element_type=f32).reshape(listed, block, LANES)
            dvs[part] = jnp.dot(low, d2, preferred_element_type=f32).reshape(listed, block, LANES)
        out_copy(2, p).start()
        for a, slots in enumerate((dks, dvs)):
            for w in range(windows):
                value = None
                for b in range(blocks):
                    if 0 <= w - b <= 2 * reach:
                        term = slots[inv[b, w - b]]
                        value = term if value is None else value + term
                piece, part = w // blocks, pl.ds((w % blocks) * block, block)
                if piece == REACH_DEV:
                    own[p, a, part, :] = value
                else:
                    far[p, piece - (piece > REACH_DEV), a, part, :] = value.astype(bf16)
        ret_one(p)
        gwp[cols, :] = lax.dot_general(
            att_v[:, cols], g_v[...], first_dim, preferred_element_type=f32
        ).astype(bf16)
        gw_one(p)

    def step(p):
        kv_wait(p)
        w_wait(p)
        attend(p)

    w_hops(jnp.int32(-4))
    for p in range(1, AHEAD_KV):
        kv_start(p)
    setup()
    w_hops(jnp.int32(-3))
    kv_first(0)
    w_hops(jnp.int32(-2))
    kv_first(1)
    w_hops(jnp.int32(-1))
    kv_second(0)
    kv_first(2)
    over(0, pairs, step)
    done = jnp.int32(pairs)
    ret_two(done - 1)
    ret_three(done - 3)
    gw_two(done - 1)
    gw_hops(done)
    ret_three(done - 2)
    mix_v[...] = jnp.dot(att_v[...], wbuf[...], preferred_element_type=f32).astype(bf16)
    pltpu.make_async_copy(mix_v, mixed_hbm, fin_sem.at[0]).start()
    gw_hops(done + 1)
    ret_three(done - 1)
    gw_hops(done + 2)
    ret_four(done - 6)
    ret_four(done - 5)
    gw_hops(done + 3)
    ret_four(done - 4)
    gw_hops(done + 4)
    gw_hops(done + 5)
    gw_hops(done + 6)
    ret_four(done - 3)
    ret_four(done - 2)
    ret_four(done - 1)

    gw_y().wait_recv()
    gwout[...] = (gfin[...] + ybuf[...].astype(f32)) * jnp.float32(1.0 / math.sqrt(tokens))
    pltpu.make_async_copy(gwout, gw_hbm, fin_sem.at[1]).start()

    w_y().wait_send()

    def sent(p):
        for a in range(2):
            kv_y(a, p).wait_send()
            kv_c(a, p).wait_send()
        pl.when(has_ahead)(lambda: kv_z(p).wait_send())
        pl.when(on_sent)(lambda: kv_on(p).wait_send())
        pl.when(sent_back)(lambda: back(p).wait_send())
        across(p).wait_send()
        pl.when(has_behind)(lambda: ret_z(p).wait_send())
        ret_y(p).wait_send()
        for a in range(3):
            out_copy(a, p).wait()
        for i in range(chips):
            chip = p * chips + i
            up, down = w_goes(chip)
            pl.when(up)(lambda chip=chip: w_z(chip, 1).wait_send())
            pl.when(down)(lambda chip=chip: w_z(chip, 0).wait_send())
            w_c(chip).wait_send()
            gw_c(chip).wait_send()
            pl.when(chip // 2 != z)(lambda chip=chip: gw_z(chip).wait_send())

    over(0, pairs, sent)
    gw_y().wait_send()
    pltpu.make_async_copy(mix_v, mixed_hbm, fin_sem.at[0]).wait()
    pltpu.make_async_copy(gwout, gw_hbm, fin_sem.at[1]).wait()


def layer(contacts, count, ids, queries, keys, values, weight, grad_output):
    n = lax.axis_size("ctx")
    rows, width = queries.shape
    blocks, listed = contacts.shape
    block = rows // blocks
    wrows = weight.shape[0]
    pairs = width // LANES
    window = (2 * REACH_DEV + 1) * blocks
    f32, bf16 = jnp.float32, jnp.bfloat16
    vmem, dma = pltpu.VMEM, pltpu.SemaphoreType.DMA
    smem = pl.BlockSpec(memory_space=pltpu.SMEM)
    hbm = pl.BlockSpec(memory_space=pl.ANY)
    slots = blocks * listed + 1
    flat, both = (rows, width), (pairs, 2, rows, LANES)
    return pl.pallas_call(
        functools.partial(layer_kernel, n, blocks, listed, block, width // HEADS, rows * n),
        in_specs=[smem, smem, pl.BlockSpec(memory_space=pltpu.VMEM)] + [hbm] * 5,
        out_specs=[hbm] * 5,
        out_shape=[jax.ShapeDtypeStruct(flat, bf16)] * 4 + [jax.ShapeDtypeStruct((wrows, width), f32)],
        scratch_shapes=[vmem(flat, bf16)] * 4
        + [
            vmem((width, width), bf16),
            vmem((pairs, 2 * REACH_DEV, 2, rows, LANES), bf16),
            vmem((window, block, block), f32),
            vmem((blocks * listed * block, LANES), f32),
            vmem((window, block, LANES), bf16),
            vmem((window, block, LANES), bf16),
            vmem((listed * block, LANES), bf16),
            vmem((listed * block, LANES), bf16),
            vmem((slots, block, LANES), f32),
            vmem((slots, block, LANES), f32),
            vmem(both, f32),
            vmem((pairs, 2 * REACH_DEV, 2, rows, LANES), bf16),
        ]
        + [vmem(both, bf16)] * 7
        + [
            vmem((pairs, rows, LANES), bf16),
            vmem(flat, bf16),
            vmem(flat, bf16),
            vmem((width, width), bf16),
            vmem((n // 2, wrows, width), bf16),
            vmem((n // 2, wrows, width), bf16),
            vmem((2, n // 2, wrows, width), bf16),
            vmem((wrows, width), bf16),
            vmem((wrows, width), bf16),
            vmem((wrows, width), f32),
            vmem((wrows, width), f32),
            pltpu.SMEM((blocks, 2 * REACH_DEV * blocks + 1), jnp.int32),
            dma((5,)),
        ]
        + [dma((2, pairs))] * 4
        + [dma((pairs,))] * 4
        + [dma, dma((2, n // 2))]
        + [dma((n // 2,))] * 3
        + [dma((4, pairs))] * 2
        + [dma((n // 2,))] * 3
        + [dma((2, n // 2)), dma, dma, dma((3, pairs)), dma((2,))],
        compiler_params=pltpu.CompilerParams(
            collective_id=0, has_side_effects=True, vmem_limit_bytes=60 * 1024 * 1024
        ),
        name="contact_layer",
    )(contacts, count, ids, queries, keys, values, weight, grad_output)


def hand_over_kernel(*refs):
    for src, dst in zip(refs[: len(refs) // 2], refs[len(refs) // 2 :]):
        dst[...] = src[...]


def hand_over(arrays, parts=2):
    specs = [pl.BlockSpec((a.shape[0] // parts, a.shape[1]), lambda i: (i, 0)) for a in arrays]
    return pl.pallas_call(
        hand_over_kernel,
        grid=(parts,),
        in_specs=specs,
        out_specs=specs,
        out_shape=[jax.ShapeDtypeStruct(a.shape, a.dtype) for a in arrays],
        name="hand_over",
    )(*arrays)


def shards(queries, keys, values, out_weight, grad_output, complex_id, contacts, contact_count):
    block = queries.shape[0] // contacts.shape[0]
    return hand_over(
        layer(contacts, contact_count, complex_id.reshape(-1, block), queries, keys, values, out_weight, grad_output)
    )


def solution(mesh):
    split = P(("groups", "ctx"), None)
    return jax.shard_map(
        shards,
        mesh=mesh,
        in_specs=(split, split, split, P("ctx", None), split, P("groups"), split, P(("groups", "ctx"))),
        out_specs=(split,) * 5,
        check_vma=False,
    )
```

```python
import functools
import math

import jax
import jax.numpy as jnp
from jax import lax
from jax.experimental import pallas as pl
from jax.experimental.pallas import tpu as pltpu
from jax.sharding import PartitionSpec as P

HEADS = 16
REACH_DEV = 2
LANES = 128
AHEAD_KV = 5


def layer_kernel(
    n, blocks, listed, block, head_dim, tokens,
    contacts, count, ids, q_hbm, k_hbm, v_hbm, w_hbm, g_hbm,
    mixed_hbm, dq_hbm, dk_hbm, dv_hbm, gw_hbm,
    q_v, k_v, v_v, g_v, wbuf, land, idt, bias, kwin, vwin, kg, vg, dks, dvs,
    own, far, got_f, got_c, got_z, got_y, put_z, put_y, outg, dqb, att_v, mix_v,
    gwp, core_got, gsum, gin, ysend, ybuf, gfin, gwout, inv,
    local_sem, y_s, y_r, c_s, c_r, z_s, z_r, o_s, o_r,
    wy_s, w_s, w_r, wc_s, wc_r, ret_s, ret_r, gc_s, gc_r, gz_s, gz_r, gy_s, gy_r,
    out_sem, fin_sem,
):
    f32, bf16 = jnp.float32, jnp.bfloat16
    rows = blocks * block
    width = q_hbm.shape[1]
    pairs = width // LANES
    wrows = w_hbm.shape[0]
    nz = n // 4
    chips = LANES // (2 * wrows)
    reach = REACH_DEV * blocks
    windows = (2 * REACH_DEV + 1) * blocks
    scale = 1.0 / math.sqrt(head_dim)

    me = lax.axis_index("ctx")
    core, y, z = lax.rem(me, 2), lax.rem(me // 2, 2), me // 4
    ypeer, cpeer = me + 2 - 4 * y, me + 1 - 2 * core
    ahead, behind = me + 4 - 8 * y, me - 4 + 8 * y
    has_ahead = (ahead >= 0) & (ahead < n)
    has_behind = (behind >= 0) & (behind < n)

    def remote(src, dst, send, recv, device):
        return pltpu.make_async_remote_copy(
            src_ref=src, dst_ref=dst, send_sem=send, recv_sem=recv,
            device_id={"ctx": device}, device_id_type=pl.DeviceIdType.MESH,
        )

    def over(start, stop, body):
        lax.fori_loop(start, stop, lambda i, c: (body(i), c)[1], 0)

    def turn(p):
        return p + 2 - 4 * lax.rem(p // 2, 2)

    def lanes(p):
        return pl.ds(pl.multiple_of(turn(p) * LANES, LANES), LANES)

    def shard(d):
        return pl.ds(pl.multiple_of(d * wrows, wrows), wrows)

    def kv_y(a, p):
        return remote(
            (k_hbm, v_hbm)[a].at[:, lanes(p)], land.at[p, 3 * y, a], y_s.at[a, p], y_r.at[a, p], ypeer
        )

    def kv_c(a, p):
        return remote(
            (k_hbm, v_hbm)[a].at[:, lanes(p)], land.at[p, 1 + core, a], c_s.at[a, p], c_r.at[a, p], cpeer
        )

    def kv_z(p):
        return remote(land.at[p, 3 - 3 * y], land.at[p, 3 * y], z_s.at[p], z_r.at[p], ahead)

    def kv_on(p):
        return remote(land.at[p, 3 - 3 * core], land.at[p, 2 - core], o_s.at[p], o_r.at[p], cpeer)

    on_sent = (y == core) | has_behind
    on_got = (y != core) | has_behind

    def kv_start(p):
        for a in range(2):
            kv_y(a, p).start()
        for a in range(2):
            kv_c(a, p).start()

    def kv_first(p):
        for a in range(2):
            kv_y(a, p).wait_recv()
        pl.when(has_ahead)(lambda: kv_z(p).start())
        pl.when(y == core)(lambda: kv_on(p).start())

    def kv_second(p):
        @pl.when(has_behind)
        def _():
            kv_z(p).wait_recv()
            pl.when(y != core)(lambda: kv_on(p).start())

    def kv_wait(p):
        for a in range(2):
            kv_c(a, p).wait_recv()
        pl.when(on_got)(lambda: kv_on(p).wait_recv())

    mychip = me // 2

    def w_y():
        return remote(w_hbm, wbuf.at[shard(me)], wy_s, w_r.at[mychip], ypeer)

    def w_in(chip):
        d = shard(2 * chip + core)
        return remote(wbuf.at[d], wbuf.at[d], wy_s, w_r.at[chip], ypeer)

    def w_z(chip, up):
        d = shard(2 * chip + core)
        return remote(wbuf.at[d], wbuf.at[d], w_s.at[up, chip], w_r.at[chip], me - 4 + 8 * up)

    def w_c(chip):
        d = shard(2 * chip + core)
        return remote(wbuf.at[d], wbuf.at[d], wc_s.at[chip], wc_r.at[chip], cpeer)

    def w_goes(chip):
        zc = chip // 2
        return (z >= zc) & (z + 1 < nz), (z <= zc) & (z > 0)

    def w_hops(now, start=0):
        def visit(q):
            for i in range(chips):
                chip = turn(q) * chips + i
                far_off = jnp.minimum(jnp.abs(z - chip // 2), 3)
                late = jnp.where(q < 1, jnp.minimum(far_off, 2) - 3, jnp.where(q < 4, far_off - 2, 2 * far_off - 3))
                late = jnp.where(q < 6, late, 2 * far_off - 1)
                near = jnp.where(q < 1, -3, jnp.where(q < 4, -2, -1))
                near = jnp.where(chip == mychip, -4, near)

                @pl.when(jnp.where(far_off == 0, near, late) == now)
                def _(chip=chip):
                    up, down = w_goes(chip)
                    pl.when(chip != mychip)(lambda: w_in(chip).wait_recv())
                    pl.when(up)(lambda: w_z(chip, 1).start())
                    pl.when(down)(lambda: w_z(chip, 0).start())
                    w_c(chip).start()

        over(start, pairs, visit)

    def w_wait(p):
        for i in range(chips):
            w_c(turn(p) * chips + i).wait_recv()

    def back(p):
        return remote(far.at[p, 1 + core], got_f.at[p], ret_s.at[0, p], ret_r.at[0, p], cpeer)

    def across(p):
        return remote(far.at[p, 2 - core], got_c.at[p], ret_s.at[1, p], ret_r.at[1, p], cpeer)

    def ret_z(p):
        return remote(put_z.at[p], got_z.at[p], ret_s.at[2, p], ret_r.at[2, p], behind)

    def ret_y(p):
        return remote(put_y.at[p], got_y.at[p], ret_s.at[3, p], ret_r.at[3, p], ypeer)

    sent_back = (y != core) | has_behind
    got_back = (y == core) | has_behind

    def ret_one(p):
        pl.when(sent_back)(lambda: back(p).start())
        across(p).start()

    def ret_two(p):
        pl.when(got_back)(lambda: back(p).wait_recv())
        value = far[p, 3 * y].astype(f32)
        put_z[p] = (value + jnp.where(y != core, got_f[p].astype(f32), 0.0)).astype(bf16)
        pl.when(has_behind)(lambda: ret_z(p).start())

    def ret_three(p):
        pl.when(has_ahead)(lambda: ret_z(p).wait_recv())
        value = far[p, 3 - 3 * y].astype(f32)
        value = value + jnp.where(has_ahead, got_z[p].astype(f32), 0.0)
        value = value + jnp.where(y == core, got_f[p].astype(f32), 0.0)
        put_y[p] = value.astype(bf16)
        ret_y(p).start()

    def out_copy(a, p):
        src = dqb.at[p] if a == 2 else outg.at[p, a]
        return pltpu.make_async_copy(src, (dk_hbm, dv_hbm, dq_hbm)[a].at[:, lanes(p)], out_sem.at[a, p])

    def ret_four(p):
        across(p).wait_recv()
        ret_y(p).wait_recv()
        outg[p] = (own[p] + got_c[p].astype(f32) + got_y[p].astype(f32)).astype(bf16)
        for a in range(2):
            out_copy(a, p).start()

    def gw_c(chip):
        return remote(
            gwp.at[shard(2 * chip + 1 - core)], core_got.at[chip], gc_s.at[chip], gc_r.at[chip], cpeer
        )

    def gw_z(chip):
        side = (z > chip // 2).astype(jnp.int32)
        return remote(
            gsum.at[chip], gin.at[side, chip], gz_s.at[chip], gz_r.at[side, chip], me + 4 - 8 * side
        )

    def gw_in(chip, side):
        return remote(gsum.at[chip], gin.at[side, chip], gz_s.at[chip], gz_r.at[side, chip], ypeer)

    def gw_y():
        return remote(ysend, ybuf, gy_s, gy_r, ypeer)

    def gw_one(p):
        for i in range(chips):
            gw_c(turn(p) * chips + i).start()

    def gw_two(p):
        for i in range(chips):
            chip = turn(p) * chips + i
            zc = chip // 2
            gw_c(chip).wait_recv()
            value = gwp[shard(2 * chip + core), :].astype(f32) + core_got[chip].astype(f32)
            gsum[chip] = value.astype(bf16)
            ends = ((z == 0) & (zc > 0)) | ((z == nz - 1) & (zc < nz - 1))
            pl.when(ends)(lambda chip=chip: gw_z(chip).start())

    def gw_hop(p, lag):
        for i in range(chips):
            chip = turn(p) * chips + i
            zc = chip // 2
            stage = jnp.where(z < zc, z, nz - 1 - z)

            @pl.when((z != zc) & (stage > 0) & (2 * jnp.minimum(stage, 2) + 1 == lag))
            def _(chip=chip, zc=zc):
                side = (z > zc).astype(jnp.int32)
                gw_in(chip, side).wait_recv()
                gsum[chip] = (gsum[chip].astype(f32) + gin[side, chip].astype(f32)).astype(bf16)
                gw_z(chip).start()

            @pl.when((z == zc) & (2 * jnp.minimum(jnp.maximum(zc, nz - 1 - zc), 3) + 1 == lag))
            def _(chip=chip):
                yc = lax.rem(chip, 2)
                pl.when(z > 0)(lambda: gw_in(chip, 0).wait_recv())
                pl.when(z < nz - 1)(lambda: gw_in(chip, 1).wait_recv())
                value = gsum[chip].astype(f32)
                value = value + jnp.where(z > 0, gin[0, chip].astype(f32), 0.0)
                value = value + jnp.where(z < nz - 1, gin[1, chip].astype(f32), 0.0)

                @pl.when(yc == y)
                def _():
                    gfin[...] = value

                @pl.when(yc != y)
                def _():
                    ysend[...] = value.astype(bf16)
                    gw_y().start()

    barrier = pltpu.get_barrier_semaphore()

    def hello(device):
        pl.semaphore_signal(barrier, inc=1, device_id={"ctx": device}, device_id_type=pl.DeviceIdType.MESH)

    hello(ypeer)
    hello(cpeer)
    pl.when(z > 0)(lambda: hello(me - 4))
    pl.when(z < nz - 1)(lambda: hello(me + 4))
    pl.semaphore_wait(barrier, 2 + (z > 0).astype(jnp.int32) + (z < nz - 1).astype(jnp.int32))

    def urgent(p):
        return mychip // chips == turn(p)

    loads = [
        pltpu.make_async_copy(w_hbm, wbuf.at[shard(me)], local_sem.at[0]),
        pltpu.make_async_copy(g_hbm, g_v, local_sem.at[1]),
        pltpu.make_async_copy(q_hbm, q_v, local_sem.at[2]),
        pltpu.make_async_copy(k_hbm, k_v, local_sem.at[3]),
        pltpu.make_async_copy(v_hbm, v_v, local_sem.at[4]),
    ]
    loads[0].start()
    pl.when(urgent(0))(lambda: w_y().start())
    kv_start(0)
    pl.when(jnp.logical_not(urgent(0)))(lambda: w_y().start())
    for copy in loads[1:]:
        copy.start()
    loads[0].wait()

    first = me * blocks - reach

    def setup():
        total_blocks = ids.shape[0]
        for w in range(windows):
            at = jnp.clip(first + w, 0, total_blocks - 1)
            row = ids[pl.ds(at, 1), :].astype(f32)
            idt[w] = jnp.broadcast_to(row, (block, block)).T
        local = [[jnp.clip(contacts[b, j] - first, 0, windows - 1) for j in range(listed)] for b in range(blocks)]
        for b in range(blocks):
            mine = ids[pl.ds(me * blocks + b, 1), :].astype(f32)
            for j in range(listed):
                same = idt[local[b][j]] == mine
                alive = jnp.full((block, LANES), count[b], jnp.int32) > j
                bias[pl.ds((b * listed + j) * block, block), :] = jnp.where(same & alive, 0.0, -jnp.inf)
            for w in range(2 * reach + 1):
                slot = jnp.int32(blocks * listed)
                for j in range(listed):
                    slot = jnp.where(local[b][j] == w + b, b * listed + j, slot)
                inv[b, w] = slot
        for ref in (dks, dvs):
            ref[blocks * listed] = jnp.zeros((block, LANES), f32)
        for copy in loads[1:]:
            copy.wait()

    lane = lax.broadcasted_iota(jnp.int32, (block, LANES), 1) < head_dim
    sub = lax.broadcasted_iota(jnp.int32, (LANES, block), 0) < head_dim
    last_dim = (((1,), (1,)), ((), ()))
    first_dim = (((0,), (0,)), ((), ()))

    def two(x):
        zero = jnp.zeros_like(x)
        return jnp.concatenate([jnp.where(lane, x, zero), jnp.where(lane, zero, x)], axis=0).astype(bf16)

    def among(q, body):
        pl.when((q >= 0) & (q < pairs))(lambda: body(q))

    def gw_hops(p):
        for lag in (3, 5, 7):
            among(p - lag, lambda q, lag=lag: gw_hop(q, lag))

    def serve(p):
        among(p + AHEAD_KV, kv_start)
        among(p - 1, ret_two)
        among(p + 3, kv_first)
        among(p - 3, ret_three)
        among(p + 1, kv_second)
        pl.when((p == 0) | ((p < 6) & (lax.rem(p, 2) == 1)))(lambda: w_hops(p, 1))
        among(p - 1, gw_two)
        gw_hops(p)
        among(p - 6, ret_four)

    def attend(p):
        cols = lanes(p)
        grad_all = lax.dot_general(
            g_v[...], wbuf[cols, :], last_dim, preferred_element_type=f32
        ).astype(bf16)
        for i, piece in enumerate((0, 1, None, 2, 3)):
            span = pl.ds(i * blocks, blocks)
            kwin[span] = (k_v[:, cols] if piece is None else land[p, piece, 0]).reshape(blocks, block, LANES)
            vwin[span] = (v_v[:, cols] if piece is None else land[p, piece, 1]).reshape(blocks, block, LANES)
        for b in range(blocks):
            if b == blocks - 1:
                serve(p)
            here = pl.ds(b * block, block)
            for j in range(listed):
                at = jnp.clip(contacts[b, j] - first, 0, windows - 1)
                kg[pl.ds(j * block, block), :] = kwin[at]
                vg[pl.ds(j * block, block), :] = vwin[at]
            grad = grad_all[b * block : (b + 1) * block].astype(f32)
            q2 = two(q_v[here, cols].astype(f32) * scale)
            d2 = two(grad)
            s = lax.dot_general(kg[...], q2, last_dim, preferred_element_type=f32)
            mask = bias[pl.ds(b * listed * block, listed * block), :]
            s = s + jnp.concatenate([mask, mask], axis=1)
            top = jnp.max(s, axis=0, keepdims=True)
            e = jnp.exp(s - top)
            probs = e * (1.0 / jnp.sum(e, axis=0, keepdims=True))
            low = probs.astype(bf16)
            ot = lax.dot_general(vg[...], low, first_dim, preferred_element_type=f32)
            att = jnp.where(sub, ot[:, :block], ot[:, block:]).astype(bf16).astype(f32)
            att_v[here, cols] = att.T.astype(bf16)
            prod = grad.T * att
            row_dot = jnp.concatenate(
                [jnp.sum(prod[:head_dim], axis=0, keepdims=True), jnp.sum(prod[head_dim:], axis=0, keepdims=True)],
                axis=1,
            )
            dp = lax.dot_general(vg[...], d2, last_dim, preferred_element_type=f32)
            ds = (probs * (dp - row_dot)).astype(bf16)
            dqt = lax.dot_general(kg[...], ds, first_dim, preferred_element_type=f32)
            dq = jnp.where(sub, dqt[:, :block], dqt[:, block:]) * scale
            dqb[p, here, :] = dq.T.astype(bf16)
            part = pl.ds(b * listed, listed)
            dks[part] = jnp.dot(ds, q2, preferred_element_type=f32).reshape(listed, block, LANES)
            dvs[part] = jnp.dot(low, d2, preferred_element_type=f32).reshape(listed, block, LANES)
        out_copy(2, p).start()
        for a, slots in enumerate((dks, dvs)):
            for w in range(windows):
                value = None
                for b in range(blocks):
                    if 0 <= w - b <= 2 * reach:
                        term = slots[inv[b, w - b]]
                        value = term if value is None else value + term
                piece, part = w // blocks, pl.ds((w % blocks) * block, block)
                if piece == REACH_DEV:
                    own[p, a, part, :] = value
                else:
                    far[p, piece - (piece > REACH_DEV), a, part, :] = value.astype(bf16)
        ret_one(p)
        gwp[cols, :] = lax.dot_general(
            att_v[:, cols], g_v[...], first_dim, preferred_element_type=f32
        ).astype(bf16)
        gw_one(p)

    def step(p):
        kv_wait(p)
        w_wait(p)
        attend(p)

    w_hops(jnp.int32(-4))
    for p in range(1, AHEAD_KV):
        kv_start(p)
    setup()
    w_hops(jnp.int32(-3))
    kv_first(0)
    w_hops(jnp.int32(-2))
    kv_first(1)
    w_hops(jnp.int32(-1))
    kv_second(0)
    kv_first(2)
    over(0, pairs, step)
    done = jnp.int32(pairs)
    ret_two(done - 1)
    ret_three(done - 3)
    gw_two(done - 1)
    gw_hops(done)
    ret_three(done - 2)
    mix_v[...] = jnp.dot(att_v[...], wbuf[...], preferred_element_type=f32).astype(bf16)
    pltpu.make_async_copy(mix_v, mixed_hbm, fin_sem.at[0]).start()
    gw_hops(done + 1)
    ret_three(done - 1)
    gw_hops(done + 2)
    ret_four(done - 6)
    ret_four(done - 5)
    gw_hops(done + 3)
    ret_four(done - 4)
    gw_hops(done + 4)
    gw_hops(done + 5)
    gw_hops(done + 6)
    ret_four(done - 3)
    ret_four(done - 2)
    ret_four(done - 1)

    gw_y().wait_recv()
    gwout[...] = (gfin[...] + ybuf[...].astype(f32)) * jnp.float32(1.0 / math.sqrt(tokens))
    pltpu.make_async_copy(gwout, gw_hbm, fin_sem.at[1]).start()

    w_y().wait_send()

    def sent(p):
        for a in range(2):
            kv_y(a, p).wait_send()
            kv_c(a, p).wait_send()
        pl.when(has_ahead)(lambda: kv_z(p).wait_send())
        pl.when(on_sent)(lambda: kv_on(p).wait_send())
        pl.when(sent_back)(lambda: back(p).wait_send())
        across(p).wait_send()
        pl.when(has_behind)(lambda: ret_z(p).wait_send())
        ret_y(p).wait_send()
        for a in range(3):
            out_copy(a, p).wait()
        for i in range(chips):
            chip = p * chips + i
            up, down = w_goes(chip)
            pl.when(up)(lambda chip=chip: w_z(chip, 1).wait_send())
            pl.when(down)(lambda chip=chip: w_z(chip, 0).wait_send())
            w_c(chip).wait_send()
            gw_c(chip).wait_send()
            pl.when(chip // 2 != z)(lambda chip=chip: gw_z(chip).wait_send())

    over(0, pairs, sent)
    gw_y().wait_send()
    pltpu.make_async_copy(mix_v, mixed_hbm, fin_sem.at[0]).wait()
    pltpu.make_async_copy(gwout, gw_hbm, fin_sem.at[1]).wait()


def layer(contacts, count, ids, queries, keys, values, weight, grad_output):
    n = lax.axis_size("ctx")
    rows, width = queries.shape
    blocks, listed = contacts.shape
    block = rows // blocks
    wrows = weight.shape[0]
    pairs = width // LANES
    window = (2 * REACH_DEV + 1) * blocks
    f32, bf16 = jnp.float32, jnp.bfloat16
    vmem, dma = pltpu.VMEM, pltpu.SemaphoreType.DMA
    smem = pl.BlockSpec(memory_space=pltpu.SMEM)
    hbm = pl.BlockSpec(memory_space=pl.ANY)
    slots = blocks * listed + 1
    flat, both = (rows, width), (pairs, 2, rows, LANES)
    return pl.pallas_call(
        functools.partial(layer_kernel, n, blocks, listed, block, width // HEADS, rows * n),
        in_specs=[smem, smem, pl.BlockSpec(memory_space=pltpu.VMEM)] + [hbm] * 5,
        out_specs=[hbm] * 5,
        out_shape=[jax.ShapeDtypeStruct(flat, bf16)] * 4 + [jax.ShapeDtypeStruct((wrows, width), f32)],
        scratch_shapes=[vmem(flat, bf16)] * 4
        + [
            vmem((width, width), bf16),
            vmem((pairs, 2 * REACH_DEV, 2, rows, LANES), bf16),
            vmem((window, block, block), f32),
            vmem((blocks * listed * block, LANES), f32),
            vmem((window, block, LANES), bf16),
            vmem((window, block, LANES), bf16),
            vmem((listed * block, LANES), bf16),
            vmem((listed * block, LANES), bf16),
            vmem((slots, block, LANES), f32),
            vmem((slots, block, LANES), f32),
            vmem(both, f32),
            vmem((pairs, 2 * REACH_DEV, 2, rows, LANES), bf16),
        ]
        + [vmem(both, bf16)] * 7
        + [
            vmem((pairs, rows, LANES), bf16),
            vmem(flat, bf16),
            vmem(flat, bf16),
            vmem((width, width), bf16),
            vmem((n // 2, wrows, width), bf16),
            vmem((n // 2, wrows, width), bf16),
            vmem((2, n // 2, wrows, width), bf16),
            vmem((wrows, width), bf16),
            vmem((wrows, width), bf16),
            vmem((wrows, width), f32),
            vmem((wrows, width), f32),
            pltpu.SMEM((blocks, 2 * REACH_DEV * blocks + 1), jnp.int32),
            dma((5,)),
        ]
        + [dma((2, pairs))] * 4
        + [dma((pairs,))] * 4
        + [dma, dma((2, n // 2))]
        + [dma((n // 2,))] * 3
        + [dma((4, pairs))] * 2
        + [dma((n // 2,))] * 3
        + [dma((2, n // 2)), dma, dma, dma((3, pairs)), dma((2,))],
        compiler_params=pltpu.CompilerParams(
            collective_id=0, has_side_effects=True, vmem_limit_bytes=60 * 1024 * 1024
        ),
        name="contact_layer",
    )(contacts, count, ids, queries, keys, values, weight, grad_output)


def hand_over_kernel(count, *refs):
    held, sems = refs[2 * count : -1], refs[-1]
    reads = [pltpu.make_async_copy(refs[i], held[i], sems.at[0, i]) for i in range(count)]
    writes = [pltpu.make_async_copy(held[i], refs[count + i], sems.at[1, i]) for i in range(count)]
    for copy in reads:
        copy.start()
    for read, write in zip(reads, writes):
        read.wait()
        write.start()
    for copy in writes:
        copy.wait()


def hand_over(arrays):
    hbm = pl.BlockSpec(memory_space=pl.ANY)
    return pl.pallas_call(
        functools.partial(hand_over_kernel, len(arrays)),
        in_specs=[hbm] * len(arrays),
        out_specs=[hbm] * len(arrays),
        out_shape=[jax.ShapeDtypeStruct(a.shape, a.dtype) for a in arrays],
        scratch_shapes=[pltpu.VMEM(a.shape, a.dtype) for a in arrays] + [pltpu.SemaphoreType.DMA((2, len(arrays)))],
        name="hand_over",
    )(*arrays)


def shards(queries, keys, values, out_weight, grad_output, complex_id, contacts, contact_count):
    block = queries.shape[0] // contacts.shape[0]
    return hand_over(
        layer(contacts, contact_count, complex_id.reshape(-1, block), queries, keys, values, out_weight, grad_output)
    )


def solution(mesh):
    split = P(("groups", "ctx"), None)
    return jax.shard_map(
        shards,
        mesh=mesh,
        in_specs=(split, split, split, P("ctx", None), split, P("groups"), split, P(("groups", "ctx"))),
        out_specs=(split,) * 5,
        check_vma=False,
    )
```

```python
import functools
import math

import jax
import jax.numpy as jnp
from jax import lax
from jax.experimental import pallas as pl
from jax.experimental.pallas import tpu as pltpu
from jax.sharding import PartitionSpec as P

HEADS = 16
REACH_DEV = 2
LANES = 128
AHEAD_KV = 5


def layer_kernel(
    n, blocks, listed, block, head_dim, tokens,
    contacts, count, ids, q_hbm, k_hbm, v_hbm, w_hbm, g_hbm,
    mixed_hbm, dq_hbm, dk_hbm, dv_hbm, gw_hbm,
    q_v, k_v, v_v, g_v, wbuf, land, idt, bias, kwin, vwin, kg, vg, dks, dvs,
    own, far, got_f, got_c, got_z, got_y, put_z, put_y, outg, dqb, att_v, mix_v,
    gwp, core_got, gsum, gin, ysend, ybuf, gfin, gwout, inv,
    local_sem, y_s, y_r, c_s, c_r, z_s, z_r, o_s, o_r,
    wy_s, w_s, w_r, wc_s, wc_r, ret_s, ret_r, gc_s, gc_r, gz_s, gz_r, gy_s, gy_r,
    out_sem, fin_sem,
):
    f32, bf16 = jnp.float32, jnp.bfloat16
    rows = blocks * block
    width = q_hbm.shape[1]
    pairs = width // LANES
    wrows = w_hbm.shape[0]
    nz = n // 4
    chips = LANES // (2 * wrows)
    reach = REACH_DEV * blocks
    windows = (2 * REACH_DEV + 1) * blocks
    scale = 1.0 / math.sqrt(head_dim)

    me = lax.axis_index("ctx")
    core, y, z = lax.rem(me, 2), lax.rem(me // 2, 2), me // 4
    ypeer, cpeer = me + 2 - 4 * y, me + 1 - 2 * core
    ahead, behind = me + 4 - 8 * y, me - 4 + 8 * y
    has_ahead = (ahead >= 0) & (ahead < n)
    has_behind = (behind >= 0) & (behind < n)

    def remote(src, dst, send, recv, device):
        return pltpu.make_async_remote_copy(
            src_ref=src, dst_ref=dst, send_sem=send, recv_sem=recv,
            device_id={"ctx": device}, device_id_type=pl.DeviceIdType.MESH,
        )

    def over(start, stop, body):
        lax.fori_loop(start, stop, lambda i, c: (body(i), c)[1], 0)

    def turn(p):
        return p + 2 - 4 * lax.rem(p // 2, 2)

    def lanes(p):
        return pl.ds(pl.multiple_of(turn(p) * LANES, LANES), LANES)

    def shard(d):
        return pl.ds(pl.multiple_of(d * wrows, wrows), wrows)

    def kv_y(a, p):
        return remote(
            (k_hbm, v_hbm)[a].at[:, lanes(p)], land.at[p, 3 * y, a], y_s.at[a, p], y_r.at[a, p], ypeer
        )

    def kv_c(a, p):
        return remote(
            (k_hbm, v_hbm)[a].at[:, lanes(p)], land.at[p, 1 + core, a], c_s.at[a, p], c_r.at[a, p], cpeer
        )

    def kv_z(a, p):
        return remote(land.at[p, 3 - 3 * y, a], land.at[p, 3 * y, a], z_s.at[a, p], z_r.at[a, p], ahead)

    def kv_on(a, p):
        return remote(land.at[p, 3 - 3 * core, a], land.at[p, 2 - core, a], o_s.at[a, p], o_r.at[a, p], cpeer)

    on_sent = (y == core) | has_behind
    on_got = (y != core) | has_behind

    def kv_start(p):
        for a in range(2):
            kv_y(a, p).start()
        for a in range(2):
            kv_c(a, p).start()

    def kv_first(p):
        for a in range(2):
            kv_y(a, p).wait_recv()
            pl.when(has_ahead)(lambda a=a: kv_z(a, p).start())
            pl.when(y == core)(lambda a=a: kv_on(a, p).start())

    def kv_second(p):
        @pl.when(has_behind)
        def _():
            for a in range(2):
                kv_z(a, p).wait_recv()
                pl.when(y != core)(lambda a=a: kv_on(a, p).start())

    def kv_wait(p):
        for a in range(2):
            kv_c(a, p).wait_recv()
            pl.when(on_got)(lambda a=a: kv_on(a, p).wait_recv())

    mychip = me // 2

    def w_y():
        return remote(w_hbm, wbuf.at[shard(me)], wy_s, w_r.at[mychip], ypeer)

    def w_in(chip):
        d = shard(2 * chip + core)
        return remote(wbuf.at[d], wbuf.at[d], wy_s, w_r.at[chip], ypeer)

    def w_z(chip, up):
        d = shard(2 * chip + core)
        return remote(wbuf.at[d], wbuf.at[d], w_s.at[up, chip], w_r.at[chip], me - 4 + 8 * up)

    def w_c(chip):
        d = shard(2 * chip + core)
        return remote(wbuf.at[d], wbuf.at[d], wc_s.at[chip], wc_r.at[chip], cpeer)

    def w_goes(chip):
        zc = chip // 2
        return (z >= zc) & (z + 1 < nz), (z <= zc) & (z > 0)

    def w_hops(now, start=0):
        def visit(q):
            for i in range(chips):
                chip = turn(q) * chips + i
                far_off = jnp.minimum(jnp.abs(z - chip // 2), 3)
                late = jnp.where(q < 1, jnp.minimum(far_off, 2) - 3, jnp.where(q < 4, far_off - 2, 2 * far_off - 3))
                late = jnp.where(q < 6, late, 2 * far_off - 1)
                near = jnp.where(q < 1, -3, jnp.where(q < 4, -2, -1))
                near = jnp.where(chip == mychip, -4, near)

                @pl.when(jnp.where(far_off == 0, near, late) == now)
                def _(chip=chip):
                    up, down = w_goes(chip)
                    pl.when(chip != mychip)(lambda: w_in(chip).wait_recv())
                    pl.when(up)(lambda: w_z(chip, 1).start())
                    pl.when(down)(lambda: w_z(chip, 0).start())
                    w_c(chip).start()

        over(start, pairs, visit)

    def w_wait(p):
        for i in range(chips):
            w_c(turn(p) * chips + i).wait_recv()

    def back(p):
        return remote(far.at[p, 1 + core], got_f.at[p], ret_s.at[0, p], ret_r.at[0, p], cpeer)

    def across(p):
        return remote(far.at[p, 2 - core], got_c.at[p], ret_s.at[1, p], ret_r.at[1, p], cpeer)

    def ret_z(p):
        return remote(put_z.at[p], got_z.at[p], ret_s.at[2, p], ret_r.at[2, p], behind)

    def ret_y(p):
        return remote(put_y.at[p], got_y.at[p], ret_s.at[3, p], ret_r.at[3, p], ypeer)

    sent_back = (y != core) | has_behind
    got_back = (y == core) | has_behind

    def ret_one(p):
        pl.when(sent_back)(lambda: back(p).start())
        across(p).start()

    def ret_two(p):
        pl.when(got_back)(lambda: back(p).wait_recv())
        value = far[p, 3 * y].astype(f32)
        put_z[p] = (value + jnp.where(y != core, got_f[p].astype(f32), 0.0)).astype(bf16)
        pl.when(has_behind)(lambda: ret_z(p).start())

    def ret_three(p):
        pl.when(has_ahead)(lambda: ret_z(p).wait_recv())
        value = far[p, 3 - 3 * y].astype(f32)
        value = value + jnp.where(has_ahead, got_z[p].astype(f32), 0.0)
        value = value + jnp.where(y == core, got_f[p].astype(f32), 0.0)
        put_y[p] = value.astype(bf16)
        ret_y(p).start()

    def out_copy(a, p):
        src = dqb.at[p] if a == 2 else outg.at[p, a]
        return pltpu.make_async_copy(src, (dk_hbm, dv_hbm, dq_hbm)[a].at[:, lanes(p)], out_sem.at[a, p])

    def ret_four(p):
        across(p).wait_recv()
        ret_y(p).wait_recv()
        outg[p] = (own[p] + got_c[p].astype(f32) + got_y[p].astype(f32)).astype(bf16)
        for a in range(2):
            out_copy(a, p).start()

    def gw_c(chip):
        return remote(
            gwp.at[shard(2 * chip + 1 - core)], core_got.at[chip], gc_s.at[chip], gc_r.at[chip], cpeer
        )

    def gw_z(chip):
        side = (z > chip // 2).astype(jnp.int32)
        return remote(
            gsum.at[chip], gin.at[side, chip], gz_s.at[chip], gz_r.at[side, chip], me + 4 - 8 * side
        )

    def gw_in(chip, side):
        return remote(gsum.at[chip], gin.at[side, chip], gz_s.at[chip], gz_r.at[side, chip], ypeer)

    def gw_y():
        return remote(ysend, ybuf, gy_s, gy_r, ypeer)

    def gw_one(p):
        for i in range(chips):
            gw_c(turn(p) * chips + i).start()

    def gw_two(p):
        for i in range(chips):
            chip = turn(p) * chips + i
            zc = chip // 2
            gw_c(chip).wait_recv()
            value = gwp[shard(2 * chip + core), :].astype(f32) + core_got[chip].astype(f32)
            gsum[chip] = value.astype(bf16)
            ends = ((z == 0) & (zc > 0)) | ((z == nz - 1) & (zc < nz - 1))
            pl.when(ends)(lambda chip=chip: gw_z(chip).start())

    def gw_hop(p, lag):
        for i in range(chips):
            chip = turn(p) * chips + i
            zc = chip // 2
            stage = jnp.where(z < zc, z, nz - 1 - z)

            @pl.when((z != zc) & (stage > 0) & (2 * jnp.minimum(stage, 2) + 1 == lag))
            def _(chip=chip, zc=zc):
                side = (z > zc).astype(jnp.int32)
                gw_in(chip, side).wait_recv()
                gsum[chip] = (gsum[chip].astype(f32) + gin[side, chip].astype(f32)).astype(bf16)
                gw_z(chip).start()

            @pl.when((z == zc) & (2 * jnp.minimum(jnp.maximum(zc, nz - 1 - zc), 3) + 1 == lag))
            def _(chip=chip):
                yc = lax.rem(chip, 2)
                pl.when(z > 0)(lambda: gw_in(chip, 0).wait_recv())
                pl.when(z < nz - 1)(lambda: gw_in(chip, 1).wait_recv())
                value = gsum[chip].astype(f32)
                value = value + jnp.where(z > 0, gin[0, chip].astype(f32), 0.0)
                value = value + jnp.where(z < nz - 1, gin[1, chip].astype(f32), 0.0)

                @pl.when(yc == y)
                def _():
                    gfin[...] = value

                @pl.when(yc != y)
                def _():
                    ysend[...] = value.astype(bf16)
                    gw_y().start()

    barrier = pltpu.get_barrier_semaphore()

    def hello(device):
        pl.semaphore_signal(barrier, inc=1, device_id={"ctx": device}, device_id_type=pl.DeviceIdType.MESH)

    hello(ypeer)
    hello(cpeer)
    pl.when(z > 0)(lambda: hello(me - 4))
    pl.when(z < nz - 1)(lambda: hello(me + 4))
    pl.semaphore_wait(barrier, 2 + (z > 0).astype(jnp.int32) + (z < nz - 1).astype(jnp.int32))

    def urgent(p):
        return mychip // chips == turn(p)

    loads = [
        pltpu.make_async_copy(w_hbm, wbuf.at[shard(me)], local_sem.at[0]),
        pltpu.make_async_copy(g_hbm, g_v, local_sem.at[1]),
        pltpu.make_async_copy(q_hbm, q_v, local_sem.at[2]),
        pltpu.make_async_copy(k_hbm, k_v, local_sem.at[3]),
        pltpu.make_async_copy(v_hbm, v_v, local_sem.at[4]),
    ]
    loads[0].start()
    pl.when(urgent(0))(lambda: w_y().start())
    kv_start(0)
    pl.when(jnp.logical_not(urgent(0)))(lambda: w_y().start())
    for copy in loads[1:]:
        copy.start()
    loads[0].wait()

    first = me * blocks - reach

    def setup():
        total_blocks = ids.shape[0]
        for w in range(windows):
            at = jnp.clip(first + w, 0, total_blocks - 1)
            row = ids[pl.ds(at, 1), :].astype(f32)
            idt[w] = jnp.broadcast_to(row, (block, block)).T
        local = [[jnp.clip(contacts[b, j] - first, 0, windows - 1) for j in range(listed)] for b in range(blocks)]
        for b in range(blocks):
            mine = ids[pl.ds(me * blocks + b, 1), :].astype(f32)
            for j in range(listed):
                same = idt[local[b][j]] == mine
                alive = jnp.full((block, LANES), count[b], jnp.int32) > j
                bias[pl.ds((b * listed + j) * block, block), :] = jnp.where(same & alive, 0.0, -jnp.inf)
            for w in range(2 * reach + 1):
                slot = jnp.int32(blocks * listed)
                for j in range(listed):
                    slot = jnp.where(local[b][j] == w + b, b * listed + j, slot)
                inv[b, w] = slot
        for ref in (dks, dvs):
            ref[blocks * listed] = jnp.zeros((block, LANES), f32)
        for copy in loads[1:]:
            copy.wait()

    lane = lax.broadcasted_iota(jnp.int32, (block, LANES), 1) < head_dim
    sub = lax.broadcasted_iota(jnp.int32, (LANES, block), 0) < head_dim
    last_dim = (((1,), (1,)), ((), ()))
    first_dim = (((0,), (0,)), ((), ()))

    def two(x):
        zero = jnp.zeros_like(x)
        return jnp.concatenate([jnp.where(lane, x, zero), jnp.where(lane, zero, x)], axis=0).astype(bf16)

    def among(q, body):
        pl.when((q >= 0) & (q < pairs))(lambda: body(q))

    def gw_hops(p):
        for lag in (3, 5, 7):
            among(p - lag, lambda q, lag=lag: gw_hop(q, lag))

    def serve(p):
        among(p + AHEAD_KV, kv_start)
        among(p - 1, ret_two)
        among(p + 3, kv_first)
        among(p - 3, ret_three)
        among(p + 1, kv_second)
        pl.when((p == 0) | ((p < 6) & (lax.rem(p, 2) == 1)))(lambda: w_hops(p, 1))
        among(p - 1, gw_two)
        gw_hops(p)
        among(p - 6, ret_four)

    def attend(p):
        cols = lanes(p)
        grad_all = lax.dot_general(
            g_v[...], wbuf[cols, :], last_dim, preferred_element_type=f32
        ).astype(bf16)
        for i, piece in enumerate((0, 1, None, 2, 3)):
            span = pl.ds(i * blocks, blocks)
            kwin[span] = (k_v[:, cols] if piece is None else land[p, piece, 0]).reshape(blocks, block, LANES)
            vwin[span] = (v_v[:, cols] if piece is None else land[p, piece, 1]).reshape(blocks, block, LANES)
        for b in range(blocks):
            if b == blocks - 1:
                serve(p)
            here = pl.ds(b * block, block)
            for j in range(listed):
                at = jnp.clip(contacts[b, j] - first, 0, windows - 1)
                kg[pl.ds(j * block, block), :] = kwin[at]
                vg[pl.ds(j * block, block), :] = vwin[at]
            grad = grad_all[b * block : (b + 1) * block].astype(f32)
            q2 = two(q_v[here, cols].astype(f32) * scale)
            d2 = two(grad)
            s = lax.dot_general(kg[...], q2, last_dim, preferred_element_type=f32)
            mask = bias[pl.ds(b * listed * block, listed * block), :]
            s = s + jnp.concatenate([mask, mask], axis=1)
            top = jnp.max(s, axis=0, keepdims=True)
            e = jnp.exp(s - top)
            probs = e * (1.0 / jnp.sum(e, axis=0, keepdims=True))
            low = probs.astype(bf16)
            ot = lax.dot_general(vg[...], low, first_dim, preferred_element_type=f32)
            att = jnp.where(sub, ot[:, :block], ot[:, block:]).astype(bf16).astype(f32)
            att_v[here, cols] = att.T.astype(bf16)
            prod = grad.T * att
            row_dot = jnp.concatenate(
                [jnp.sum(prod[:head_dim], axis=0, keepdims=True), jnp.sum(prod[head_dim:], axis=0, keepdims=True)],
                axis=1,
            )
            dp = lax.dot_general(vg[...], d2, last_dim, preferred_element_type=f32)
            ds = (probs * (dp - row_dot)).astype(bf16)
            dqt = lax.dot_general(kg[...], ds, first_dim, preferred_element_type=f32)
            dq = jnp.where(sub, dqt[:, :block], dqt[:, block:]) * scale
            dqb[p, here, :] = dq.T.astype(bf16)
            part = pl.ds(b * listed, listed)
            dks[part] = jnp.dot(ds, q2, preferred_element_type=f32).reshape(listed, block, LANES)
            dvs[part] = jnp.dot(low, d2, preferred_element_type=f32).reshape(listed, block, LANES)
        out_copy(2, p).start()
        for a, slots in enumerate((dks, dvs)):
            for w in range(windows):
                value = None
                for b in range(blocks):
                    if 0 <= w - b <= 2 * reach:
                        term = slots[inv[b, w - b]]
                        value = term if value is None else value + term
                piece, part = w // blocks, pl.ds((w % blocks) * block, block)
                if piece == REACH_DEV:
                    own[p, a, part, :] = value
                else:
                    far[p, piece - (piece > REACH_DEV), a, part, :] = value.astype(bf16)
        ret_one(p)
        gwp[cols, :] = lax.dot_general(
            att_v[:, cols], g_v[...], first_dim, preferred_element_type=f32
        ).astype(bf16)
        gw_one(p)

    def step(p):
        kv_wait(p)
        w_wait(p)
        attend(p)

    w_hops(jnp.int32(-4))
    for p in range(1, AHEAD_KV):
        kv_start(p)
    setup()
    w_hops(jnp.int32(-3))
    kv_first(0)
    w_hops(jnp.int32(-2))
    kv_first(1)
    w_hops(jnp.int32(-1))
    kv_second(0)
    kv_first(2)
    over(0, pairs, step)
    done = jnp.int32(pairs)
    ret_two(done - 1)
    ret_three(done - 3)
    gw_two(done - 1)
    gw_hops(done)
    ret_three(done - 2)
    mix_v[...] = jnp.dot(att_v[...], wbuf[...], preferred_element_type=f32).astype(bf16)
    pltpu.make_async_copy(mix_v, mixed_hbm, fin_sem.at[0]).start()
    gw_hops(done + 1)
    ret_three(done - 1)
    gw_hops(done + 2)
    ret_four(done - 6)
    ret_four(done - 5)
    gw_hops(done + 3)
    ret_four(done - 4)
    gw_hops(done + 4)
    gw_hops(done + 5)
    gw_hops(done + 6)
    ret_four(done - 3)
    ret_four(done - 2)
    ret_four(done - 1)

    gw_y().wait_recv()
    gwout[...] = (gfin[...] + ybuf[...].astype(f32)) * jnp.float32(1.0 / math.sqrt(tokens))
    pltpu.make_async_copy(gwout, gw_hbm, fin_sem.at[1]).start()

    w_y().wait_send()

    def sent(p):
        for a in range(2):
            kv_y(a, p).wait_send()
            kv_c(a, p).wait_send()
            pl.when(has_ahead)(lambda a=a: kv_z(a, p).wait_send())
            pl.when(on_sent)(lambda a=a: kv_on(a, p).wait_send())
        pl.when(sent_back)(lambda: back(p).wait_send())
        across(p).wait_send()
        pl.when(has_behind)(lambda: ret_z(p).wait_send())
        ret_y(p).wait_send()
        for a in range(3):
            out_copy(a, p).wait()
        for i in range(chips):
            chip = p * chips + i
            up, down = w_goes(chip)
            pl.when(up)(lambda chip=chip: w_z(chip, 1).wait_send())
            pl.when(down)(lambda chip=chip: w_z(chip, 0).wait_send())
            w_c(chip).wait_send()
            gw_c(chip).wait_send()
            pl.when(chip // 2 != z)(lambda chip=chip: gw_z(chip).wait_send())

    over(0, pairs, sent)
    gw_y().wait_send()
    pltpu.make_async_copy(mix_v, mixed_hbm, fin_sem.at[0]).wait()
    pltpu.make_async_copy(gwout, gw_hbm, fin_sem.at[1]).wait()


def layer(contacts, count, ids, queries, keys, values, weight, grad_output):
    n = lax.axis_size("ctx")
    rows, width = queries.shape
    blocks, listed = contacts.shape
    block = rows // blocks
    wrows = weight.shape[0]
    pairs = width // LANES
    window = (2 * REACH_DEV + 1) * blocks
    f32, bf16 = jnp.float32, jnp.bfloat16
    vmem, dma = pltpu.VMEM, pltpu.SemaphoreType.DMA
    smem = pl.BlockSpec(memory_space=pltpu.SMEM)
    hbm = pl.BlockSpec(memory_space=pl.ANY)
    slots = blocks * listed + 1
    flat, both = (rows, width), (pairs, 2, rows, LANES)
    return pl.pallas_call(
        functools.partial(layer_kernel, n, blocks, listed, block, width // HEADS, rows * n),
        in_specs=[smem, smem, pl.BlockSpec(memory_space=pltpu.VMEM)] + [hbm] * 5,
        out_specs=[hbm] * 5,
        out_shape=[jax.ShapeDtypeStruct(flat, bf16)] * 4 + [jax.ShapeDtypeStruct((wrows, width), f32)],
        scratch_shapes=[vmem(flat, bf16)] * 4
        + [
            vmem((width, width), bf16),
            vmem((pairs, 2 * REACH_DEV, 2, rows, LANES), bf16),
            vmem((window, block, block), f32),
            vmem((blocks * listed * block, LANES), f32),
            vmem((window, block, LANES), bf16),
            vmem((window, block, LANES), bf16),
            vmem((listed * block, LANES), bf16),
            vmem((listed * block, LANES), bf16),
            vmem((slots, block, LANES), f32),
            vmem((slots, block, LANES), f32),
            vmem(both, f32),
            vmem((pairs, 2 * REACH_DEV, 2, rows, LANES), bf16),
        ]
        + [vmem(both, bf16)] * 7
        + [
            vmem((pairs, rows, LANES), bf16),
            vmem(flat, bf16),
            vmem(flat, bf16),
            vmem((width, width), bf16),
            vmem((n // 2, wrows, width), bf16),
            vmem((n // 2, wrows, width), bf16),
            vmem((2, n // 2, wrows, width), bf16),
            vmem((wrows, width), bf16),
            vmem((wrows, width), bf16),
            vmem((wrows, width), f32),
            vmem((wrows, width), f32),
            pltpu.SMEM((blocks, 2 * REACH_DEV * blocks + 1), jnp.int32),
            dma((5,)),
        ]
        + [dma((2, pairs))] * 8
        + [dma, dma((2, n // 2))]
        + [dma((n // 2,))] * 3
        + [dma((4, pairs))] * 2
        + [dma((n // 2,))] * 3
        + [dma((2, n // 2)), dma, dma, dma((3, pairs)), dma((2,))],
        compiler_params=pltpu.CompilerParams(
            collective_id=0, has_side_effects=True, vmem_limit_bytes=60 * 1024 * 1024
        ),
        name="contact_layer",
    )(contacts, count, ids, queries, keys, values, weight, grad_output)


def hand_over_kernel(count, *refs):
    held, sems = refs[2 * count : -1], refs[-1]
    reads = [pltpu.make_async_copy(refs[i], held[i], sems.at[0, i]) for i in range(count)]
    writes = [pltpu.make_async_copy(held[i], refs[count + i], sems.at[1, i]) for i in range(count)]
    for copy in reads:
        copy.start()
    for read, write in zip(reads, writes):
        read.wait()
        write.start()
    for copy in writes:
        copy.wait()


def hand_over(arrays):
    hbm = pl.BlockSpec(memory_space=pl.ANY)
    return pl.pallas_call(
        functools.partial(hand_over_kernel, len(arrays)),
        in_specs=[hbm] * len(arrays),
        out_specs=[hbm] * len(arrays),
        out_shape=[jax.ShapeDtypeStruct(a.shape, a.dtype) for a in arrays],
        scratch_shapes=[pltpu.VMEM(a.shape, a.dtype) for a in arrays] + [pltpu.SemaphoreType.DMA((2, len(arrays)))],
        name="hand_over",
    )(*arrays)


def shards(queries, keys, values, out_weight, grad_output, complex_id, contacts, contact_count):
    block = queries.shape[0] // contacts.shape[0]
    return hand_over(
        layer(contacts, contact_count, complex_id.reshape(-1, block), queries, keys, values, out_weight, grad_output)
    )


def solution(mesh):
    split = P(("groups", "ctx"), None)
    return jax.shard_map(
        shards,
        mesh=mesh,
        in_specs=(split, split, split, P("ctx", None), split, P("groups"), split, P(("groups", "ctx"))),
        out_specs=(split,) * 5,
        check_vma=False,
    )
```
